1024 devices in a mesh: band: 32 (over y, x), set: 32 (over z, core).
Axes of the slice: x: 4, y: 8, z: 16, core: 2. Of those that a mesh axis runs over, the one named last changes fastest.
Arguments:
- grid: float32 [64, 5152, 128], P('band', 'set'), may hold values from -6 to 6
- row_points: int32 [64], P('band'), may hold values from 20 to 5136, as said below
- legendre: bfloat16 [640, 64, 1408], P('set'), may hold values from -0.5 to 0.5
Outputs:
- spectra: float32 [640, 1408, 128], P('set', 'band')
The draws below stay inside these ranges and needn't reach their ends.
Inputs may be any that keep to these rules, and one draw needn't show every extreme that they name: row_points[r] is 4 j + 20 for some row j of the model grid with r * (20) <= j < (r + 1) * 20; the last row has 5136 points.
All inputs are finite; a program needn't handle non-finite values.
Results may differ from the reference program's by a relative error of at most 0.0029.
Values may be sent and summed in bfloat16 or wider, within the bound.
A program may use at most 32 MiB of HBM per device.

```python
import math
import jax
import jax.numpy as jnp
from jax import lax

TRUNC = 1279
COLS = 64
WAVES = 1280
PAIRS = 640
NPAD = 1408
LATS = 64
CAP = 5152


def draw_row_points(key, part):
    row_ids = jnp.arange(LATS, dtype=jnp.int32)
    stride = WAVES // LATS
    offsets = jax.random.randint(key, (LATS,), 0, stride, dtype=jnp.int32)
    latitude = jnp.where(row_ids == LATS - 1, WAVES - 1, row_ids * stride + offsets)
    return (4 * latitude + 20).astype(jnp.int32)


def levels(stream_key, extent, pieces, least, largest):
    gain = 1.0
    for dim, parts in pieces:
        steps = jax.random.uniform(jax.random.fold_in(jax.random.fold_in(stream_key, 6), dim), (parts,), jnp.float32, least / len(pieces), largest / len(pieces))
        gain = gain * jnp.repeat(jnp.exp(steps), extent[dim] // parts).reshape((-1,) + (1,) * (len(extent) - 1 - dim))
    return gain


def normal_values(stream_key, dims, deviation, most, pieces=(), held_as=jnp.bfloat16):
    gain = levels(stream_key, dims, pieces, -0.22, 0.18) if pieces else 1.0
    entries = jax.random.normal(stream_key, dims, jnp.float32) * deviation * gain
    return jnp.minimum(jnp.maximum(entries, -most), most).astype(held_as)


def setup_inputs(seed: int = 0) -> dict:
    splits = jax.random.split(jax.random.key(seed), 4)
    return {
        "grid": normal_values(splits[0], (LATS, CAP, 2 * COLS), 1.0, 6.0, ((0, 32), (1, 32)), jnp.float32),
        "row_points": draw_row_points(jax.random.fold_in(splits[3], 71), 0),
        "legendre": normal_values(splits[2], (PAIRS, LATS, NPAD), (2 * LATS) ** -0.5, 0.5, ((0, 32),)),
    }


def reference(grid, row_points, legendre):
    waves = TRUNC + 1
    point_ids = jnp.arange(CAP, dtype=jnp.int32)
    wave_ids = jnp.arange(waves, dtype=jnp.int32)

    def row_transform(item):
        row_block, length = item
        residue = point_ids[:, None] * wave_ids[None, :] % length
        length_float = length.astype(jnp.float32)
        phases = residue.astype(jnp.float32) * (2.0 * math.pi / length_float)
        usable = (point_ids[:, None] < length) & (wave_ids[None, :] <= (length - 1) // 2)
        row_scale = lax.rsqrt(length_float)
        cosine_part = jnp.where(usable, jnp.cos(phases) * row_scale, 0.0)
        sine_part = jnp.where(usable, -jnp.sin(phases) * row_scale, 0.0)
        table = jnp.stack([cosine_part, sine_part], axis=1)
        values = row_block.reshape(CAP, 2, COLS)
        fourier = jnp.einsum('qhc,qem->mhec', values, table, precision=lax.Precision.HIGHEST)
        halves = jnp.stack([fourier[:, 0] + fourier[:, 1], fourier[:, 0] - fourier[:, 1]], axis=1)
        return halves.reshape(waves, 2, 2 * COLS).astype(jnp.bfloat16)
    halves = lax.map(row_transform, (grid, row_points))
    slot_ids = jnp.arange(NPAD, dtype=jnp.int32)
    class_ids = jnp.arange(4, dtype=jnp.int32)

    def pair_spectra(pair_id):
        legend_rows = legendre[pair_id].astype(jnp.float32)
        side_one = lax.dynamic_index_in_dim(halves, pair_id, 1, keepdims=False)
        side_two = lax.dynamic_index_in_dim(halves, TRUNC - pair_id, 1, keepdims=False)
        sources = jnp.concatenate([side_one, side_two], axis=1).astype(jnp.float32)
        products = jnp.einsum('rk,rjc->kjc', legend_rows, sources)
        is_first = slot_ids <= TRUNC - pair_id
        parity = jnp.where(is_first, slot_ids % 2, (slot_ids - 1 - TRUNC + pair_id) % 2)
        selector = jnp.where(is_first, 0, 2) + parity
        weights = (selector[:, None] == class_ids[None, :]).astype(jnp.float32)
        return lax.optimization_barrier(jnp.sum(products * weights[:, :, None], axis=1))
    return lax.map(pair_spectra, jnp.arange(PAIRS, dtype=jnp.int32))
```

```python
import functools
import math

import jax
import jax.numpy as jnp
from jax import lax
from jax.experimental import pallas as pl
from jax.experimental.pallas import tpu as pltpu
from jax.sharding import PartitionSpec as P

MESH = pl.DeviceIdType.MESH
CHIPS_X = 4
WINDOW = 256
SIN_TERMS = (1.0, -1 / 6, 1 / 120, -1 / 5040, 1 / 362880, -1 / 39916800)
COS_TERMS = (1.0, -1 / 2, 1 / 24, -1 / 720, 1 / 40320, -1 / 3628800, 1 / 479001600)


def horner(terms, square):
    total = jnp.full_like(square, terms[-1])
    for term in terms[-2::-1]:
        total = total * square + term
    return total


def cos_sin(waves, points, length):
    product = waves * points
    residue = product - jnp.floor(product * (1.0 / length) + 0.5) * length
    half = residue * (math.pi / length)
    square = half * half
    sine = half * horner(SIN_TERMS, square)
    cosine = horner(COS_TERMS, square)
    return 1.0 - 2.0 * sine * sine, 2.0 * sine * cosine


def split(value):
    high = value.astype(jnp.bfloat16)
    return high, (value - high.astype(jnp.float32)).astype(jnp.bfloat16)


def kernel(
    sizes,
    rows_ref,
    grid_ref,
    leg_ref,
    out_ref,
    twin,
    folded,
    grid_high,
    grid_low,
    window,
    leg_rows,
    weights,
    send_r,
    recv_r,
    send_l,
    recv_l,
    packed,
    blocks,
    spread,
    leg_sem,
    twin_sem,
    ring_send,
    ring_recv,
    y_send,
    y_recv,
    x_send,
    x_recv,
):
    bands, sets, nx, pairs, slots, per_device = sizes
    ny, nz = bands // nx, sets // 2
    half = nz // 2
    trunc = 2 * pairs * sets - 1
    group_rows = 2 * pairs
    band, group = lax.axis_index("band"), lax.axis_index("set")
    y, x = lax.div(band, nx), lax.rem(band, nx)
    z, core = lax.div(group, 2), lax.rem(group, 2)
    sibling = z * 2 + 1 - core

    def at_z(position):
        return lax.rem(position + nz, nz) * 2 + core

    right, left = at_z(z + 1), at_z(z - 1)

    def at_y(position):
        return lax.rem(position + ny, ny) * nx + x

    def at_x(position):
        return y * nx + lax.rem(position, nx)

    def needs(side, of_band):
        if side == 0:
            return slots * of_band <= trunc - pairs * group
        return slots * of_band + slots - 1 >= trunc + 1 - (pairs * group + pairs - 1)

    def row_needs(side, of_y):
        return needs(side, of_y * nx + (0 if side == 0 else nx - 1))

    peers = [(band, sibling), (band, right), (band, left)]
    if nz == 2:
        peers.pop()
    peers += [(at_y(y + d), group) for d in range(1, ny)]
    peers += [(at_x(x + d), group) for d in range(1, nx)]
    barrier = pltpu.get_barrier_semaphore()
    for peer in peers:
        pl.semaphore_signal(barrier, inc=1, device_id=peer, device_id_type=MESH)

    first = slots * band
    start = jnp.minimum(lax.div(first, 128) * 128, leg_ref.shape[2] - WINDOW)
    leg_copy = pltpu.make_async_copy(
        leg_ref.at[:, :, pl.ds(pl.multiple_of(start, 128), WINDOW)], window, leg_sem
    )
    leg_copy.start()

    lengths = [rows_ref[q].astype(jnp.float32) for q in range(2)]
    bases = [group * per_device, sibling * per_device]

    def prepare(source, half_index):
        for q in range(2):
            folded[q, 0:per_device, :] = source[pl.ds(q, per_device, stride=2), :]
        for q in range(2):
            value = folded[q]
            point = bases[half_index] + lax.broadcasted_iota(jnp.int32, value.shape, 0)
            lane = lax.broadcasted_iota(jnp.int32, value.shape, 1)
            other = pltpu.roll(value, 64, 1)
            value = jnp.where(lane < 64, value + other, other - value)
            value = value * lax.rsqrt(jnp.full(value.shape, lengths[q], jnp.float32))
            row = lax.broadcasted_iota(jnp.int32, value.shape, 0)
            value = jnp.where((point < rows_ref[q]) & (row < per_device), value, 0.0)
            grid_high[q, half_index], grid_low[q, half_index] = split(value)

    def partials(owners):
        count = len(owners) * group_rows
        index = lax.broadcasted_iota(jnp.int32, (count, 1), 0)
        waves = jnp.zeros((count, 1), jnp.int32)
        for position, owner in enumerate(owners):
            inside = index - position * group_rows
            here = jnp.where(
                inside < pairs, pairs * owner + inside, trunc - pairs * owner - (inside - pairs)
            )
            waves = jnp.where(inside >= 0, here, waves)
        waves = waves.astype(jnp.float32)
        lane = lax.broadcasted_iota(jnp.int32, (1, 256), 1)
        results = []
        for q in range(2):
            length = jnp.full((1, 256), lengths[q], jnp.float32)
            total = jnp.zeros((2 * count, 128), jnp.float32)
            for half_index in range(2):
                points = (bases[half_index] + lane).astype(jnp.float32)
                table = jnp.concatenate(cos_sin(waves, points, length), axis=0)
                high, low = split(table)
                for factor, values in ((high, grid_high), (low, grid_high), (high, grid_low)):
                    total = total + jnp.dot(
                        factor, values[q, half_index], preferred_element_type=jnp.float32
                    )
            results.append(total)
        return results

    def ring_copy(to_right, slot, q):
        side = 0 if to_right else 1
        source, target = (send_r, recv_r) if to_right else (send_l, recv_l)
        return pltpu.make_async_remote_copy(
            src_ref=source.at[slot, q],
            dst_ref=target.at[slot, q],
            send_sem=ring_send.at[side, slot, q],
            recv_sem=ring_recv.at[side, slot, q],
            device_id=(band, right if to_right else left),
            device_id_type=MESH,
        )

    def weights_of(pair):
        values = window[pair].astype(jnp.float32)
        values = pltpu.roll(values, lax.rem(WINDOW - (first - start), WINDOW), 1)[:, :128]
        leg_rows[...] = values
        rows = jnp.concatenate([leg_rows[pl.ds(q, bands, stride=2), :] for q in range(2)], axis=0)
        turned = jnp.transpose(rows)[: weights.shape[2]]
        turned = jnp.concatenate([turned, turned], axis=1)
        slot = first + lax.broadcasted_iota(jnp.int32, turned.shape, 0)
        parity = lax.div(lax.broadcasted_iota(jnp.int32, turned.shape, 1), 2 * bands)
        number = pairs * group + pair
        is_first = slot <= trunc - number
        even = (slot & 1) == parity
        other = ((slot - 1 - trunc + number) & 1) == parity
        weights[0, pair] = jnp.where(is_first & even, turned, 0.0).astype(jnp.bfloat16)
        weights[1, pair] = jnp.where((~is_first) & other, turned, 0.0).astype(jnp.bfloat16)

    folded[:, per_device:, :] = jnp.zeros_like(folded[:, per_device:, :])
    recv_r[0, 0] = jnp.zeros_like(recv_r[0, 0])
    recv_l[0, 1] = jnp.zeros_like(recv_l[0, 1])
    prepare(grid_ref, 0)

    pl.semaphore_wait(barrier, len(peers))
    swap = pltpu.make_async_remote_copy(
        src_ref=grid_ref,
        dst_ref=twin,
        send_sem=twin_sem.at[0],
        recv_sem=twin_sem.at[1],
        device_id=(band, sibling),
        device_id_type=MESH,
    )
    swap.start()
    swap.wait()
    prepare(twin, 1)

    far = partials([at_z(z + half)])
    send_l[0, 0] = far[0]
    ring_copy(False, 0, 0).start()
    send_r[0, 1] = far[1]
    ring_copy(True, 0, 1).start()
    leg_copy.wait()
    per_step = -(-pairs // max(half - 1, 1))

    def weights_step(step):
        def one(index, carry):
            pair = (step - 1) * per_step + index

            @pl.when(pair < pairs)
            def _():
                weights_of(pair)

            return carry

        lax.fori_loop(0, per_step, one, 0)

    def ring_step(step, carry):
        mine = partials([at_z(z + half - step), at_z(z - half + step)])
        for q in range(2):
            for to_right in (True, False):
                source, came = (send_r, recv_r) if to_right else (send_l, recv_l)

                @pl.when((step > 1) | (q == (1 if to_right else 0)))
                def _():
                    ring_copy(to_right, step - 1, q).wait_recv()

                offset = 0 if to_right else group_rows
                for part in range(2):
                    low = 2 * part * group_rows + offset
                    span = slice(part * group_rows, (part + 1) * group_rows)
                    source[step, q, span] = (
                        came[step - 1, q, span] + mine[q][low : low + group_rows]
                    )
                ring_copy(to_right, step, q).start()
        weights_step(step)
        return carry

    lax.fori_loop(1, half, ring_step, 0)
    if half == 1:
        weights_step(1)

    own = partials([group])
    last = half - 1
    for q in range(2):
        for to_right in (True, False):
            if half > 1 or q == (1 if to_right else 0):
                ring_copy(to_right, last, q).wait_recv()

    for q in range(2):
        total = own[q] + recv_r[last, q] + recv_l[last, q]
        index = lax.broadcasted_iota(jnp.int32, (group_rows, 128), 0)
        wave = jnp.where(index < pairs, pairs * group + index, trunc - pairs * group - (index - pairs))
        usable = wave <= lax.div(rows_ref[q] - 1, 2)
        cosine = jnp.where(usable, total[:group_rows], 0.0)
        sine = jnp.where(usable, -total[group_rows:], 0.0)
        lane = lax.broadcasted_iota(jnp.int32, (group_rows, 128), 1)
        parts = (
            jnp.where(lane < 64, cosine, pltpu.roll(sine, 64, 1)),
            jnp.where(lane < 64, pltpu.roll(cosine, 64, 1), sine),
        )
        for parity in range(2):
            for side in range(2):
                at = (parity * 2 + q) * pairs
                packed[side, at : at + pairs] = parts[parity][side * pairs : (side + 1) * pairs]
    for side in range(2):
        blocks[side, band] = packed[side].astype(jnp.bfloat16)

    def y_copy(side, distance):
        return pltpu.make_async_remote_copy(
            src_ref=blocks.at[side, band],
            dst_ref=blocks.at[side, band],
            send_sem=y_send.at[side, distance],
            recv_sem=y_recv.at[side, y],
            device_id=(at_y(y + distance), group),
            device_id_type=MESH,
        )

    def y_arrival(side, source_y):
        spot = blocks.at[side, source_y * nx + x]
        return pltpu.make_async_remote_copy(
            src_ref=spot,
            dst_ref=spot,
            send_sem=y_send.at[side, 0],
            recv_sem=y_recv.at[side, source_y],
            device_id=(at_y(y + 1), group),
            device_id_type=MESH,
        )

    def x_copy(side, source_y, distance):
        spot = blocks.at[side, source_y * nx + x]
        return pltpu.make_async_remote_copy(
            src_ref=spot,
            dst_ref=spot,
            send_sem=x_send.at[side, source_y, distance],
            recv_sem=x_recv.at[side, source_y * nx + x],
            device_id=(at_x(x + distance), group),
            device_id_type=MESH,
        )

    def x_arrival(side, source):
        spot = blocks.at[side, source]
        return pltpu.make_async_remote_copy(
            src_ref=spot,
            dst_ref=spot,
            send_sem=x_send.at[side, 0, 0],
            recv_sem=x_recv.at[side, source],
            device_id=(at_x(x + 1), group),
            device_id_type=MESH,
        )

    def in_turn(index):
        step = lax.div(index + 1, 2)
        return jnp.where(lax.rem(index, 2) == 1, step, ny - step)

    def y_start(index, carry):
        distance = lax.rem(in_turn(index), ny)
        for side in range(2):
            @pl.when(row_needs(side, lax.rem(y + distance, ny)))
            def _():
                y_copy(side, distance).start()

        return carry

    lax.fori_loop(1, ny, y_start, 0)

    def unpack(side, source):
        span = 4 * pairs
        spread[side, pl.ds(pl.multiple_of(source * span, 8), span), :] = blocks[
            side, source
        ].astype(jnp.float32)

    def forward(index, carry):
        source_y = lax.rem(y + in_turn(index), ny)
        for side in range(2):
            @pl.when(row_needs(side, y) & (index > 0))
            def _():
                y_arrival(side, source_y).wait_recv()

            for distance in range(1, nx):
                @pl.when(needs(side, at_x(x + distance)))
                def _():
                    x_copy(side, source_y, distance).start()

            @pl.when(needs(side, band))
            def _():
                unpack(side, source_y * nx + x)

        return carry

    lax.fori_loop(0, ny, forward, 0)

    def collect(index, carry):
        source_y = lax.rem(y + in_turn(index), ny)
        for side in range(2):
            for distance in range(1, nx):
                @pl.when(needs(side, band))
                def _():
                    source = source_y * nx + lax.rem(x + distance, nx)
                    x_arrival(side, source).wait_recv()
                    unpack(side, source)

        return carry

    lax.fori_loop(0, ny, collect, 0)

    def legendre(side, add):
        def one(pair, carry):
            parts = [
                spread[side, pl.ds((2 * parity + q) * pairs + pair, bands, stride=4 * pairs), :]
                for parity in range(2)
                for q in range(2)
            ]
            values = jnp.concatenate(parts, axis=0).astype(jnp.bfloat16)
            result = jnp.dot(weights[side, pair], values, preferred_element_type=jnp.float32)
            result = result[:slots]
            out_ref[pair] = out_ref[pair] + result if add else result
            return carry

        lax.fori_loop(0, pairs, one, 0)

    pl.when(needs(0, band))(lambda: legendre(0, False))
    pl.when(needs(1, band) & ~needs(0, band))(lambda: legendre(1, False))
    pl.when(needs(1, band) & needs(0, band))(lambda: legendre(1, True))

    for to_right in (True, False):
        for q in range(2):
            if q == (1 if to_right else 0):
                ring_copy(to_right, 0, q).wait_send()

    def ring_sent(step, carry):
        for to_right in (True, False):
            for q in range(2):
                ring_copy(to_right, step, q).wait_send()
        return carry

    lax.fori_loop(1, half, ring_sent, 0)

    def y_sent(distance, carry):
        for side in range(2):
            @pl.when(row_needs(side, lax.rem(y + distance, ny)))
            def _():
                y_copy(side, distance).wait_send()

        return carry

    lax.fori_loop(1, ny, y_sent, 0)

    def x_sent(source_y, carry):
        for side in range(2):
            for distance in range(1, nx):
                @pl.when(needs(side, at_x(x + distance)))
                def _():
                    x_copy(side, source_y, distance).wait_send()

        return carry

    lax.fori_loop(0, ny, x_sent, 0)


def shards(nx, grid, row_points, legendre):
    bands, sets = lax.axis_size("band"), lax.axis_size("set")
    pairs, rows, width = legendre.shape
    slots = width // bands
    per_device = grid.shape[1]
    points = jnp.transpose(grid, (1, 0, 2)).reshape(2 * per_device, 128)
    half = sets // 4
    padded = -(-slots // 16) * 16
    group_rows = 2 * pairs
    f32, bf16 = jnp.float32, jnp.bfloat16
    ring = pltpu.VMEM((half, 2, 2 * group_rows, 128), f32)
    return pl.pallas_call(
        functools.partial(kernel, (bands, sets, nx, pairs, slots, per_device)),
        out_shape=jax.ShapeDtypeStruct((pairs, slots, 128), f32),
        in_specs=[
            pl.BlockSpec(memory_space=pltpu.SMEM),
            pl.BlockSpec(memory_space=pltpu.VMEM),
            pl.BlockSpec(memory_space=pl.ANY),
        ],
        out_specs=pl.BlockSpec(memory_space=pltpu.VMEM),
        scratch_shapes=[
            pltpu.VMEM((2 * per_device, 128), f32),
            pltpu.VMEM((2, 256, 128), f32),
            pltpu.VMEM((2, 2, 256, 128), bf16),
            pltpu.VMEM((2, 2, 256, 128), bf16),
            pltpu.VMEM((pairs, rows, WINDOW), bf16),
            pltpu.VMEM((rows, 128), f32),
            pltpu.VMEM((2, pairs, padded, 2 * rows), bf16),
            ring,
            ring,
            ring,
            ring,
            pltpu.VMEM((2, 4 * pairs, 128), f32),
            pltpu.VMEM((2, bands, 4 * pairs, 128), bf16),
            pltpu.VMEM((2, bands * 4 * pairs, 128), f32),
            pltpu.SemaphoreType.DMA,
            pltpu.SemaphoreType.DMA((2,)),
            pltpu.SemaphoreType.DMA((2, half, 2)),
            pltpu.SemaphoreType.DMA((2, half, 2)),
            pltpu.SemaphoreType.DMA((2, bands // nx)),
            pltpu.SemaphoreType.DMA((2, bands // nx)),
            pltpu.SemaphoreType.DMA((2, bands // nx, nx)),
            pltpu.SemaphoreType.DMA((2, bands)),
        ],
        compiler_params=pltpu.CompilerParams(
            collective_id=0, has_side_effects=True, vmem_limit_bytes=40 * 1024 * 1024
        ),
    )(row_points, points, legendre)


def solution(mesh, nx=CHIPS_X):
    return jax.shard_map(
        functools.partial(shards, nx),
        mesh=mesh,
        in_specs=(P("band", "set", None), P("band"), P("set", None, None)),
        out_specs=P("set", "band", None),
        check_vma=False,
    )
```

```python
import functools
import math

import jax
import jax.numpy as jnp
from jax import lax
from jax.experimental import pallas as pl
from jax.experimental.pallas import tpu as pltpu
from jax.sharding import PartitionSpec as P

MESH = pl.DeviceIdType.MESH
CHIPS_X = 4
WINDOW = 256
SIN_TERMS = (1.0, -1 / 6, 1 / 120, -1 / 5040, 1 / 362880, -1 / 39916800)
COS_TERMS = (1.0, -1 / 2, 1 / 24, -1 / 720, 1 / 40320, -1 / 3628800, 1 / 479001600)


def horner(terms, square):
    total = jnp.full_like(square, terms[-1])
    for term in terms[-2::-1]:
        total = total * square + term
    return total


def cos_sin(waves, points, length):
    product = waves * points
    residue = product - jnp.floor(product * (1.0 / length) + 0.5) * length
    half = residue * (math.pi / length)
    square = half * half
    sine = half * horner(SIN_TERMS, square)
    cosine = horner(COS_TERMS, square)
    return 1.0 - 2.0 * sine * sine, 2.0 * sine * cosine


def split(value):
    high = value.astype(jnp.bfloat16)
    return high, (value - high.astype(jnp.float32)).astype(jnp.bfloat16)


def kernel(
    sizes,
    rows_hbm,
    grid_hbm,
    leg_ref,
    out_ref,
    rows_ref,
    mine_raw,
    twin,
    folded,
    grid_high,
    grid_low,
    window,
    leg_rows,
    weights,
    sum_out,
    sum_in,
    term_out,
    term_in,
    packed,
    blocks,
    spread,
    leg_sem,
    own_sem,
    twin_sem,
    sum_send,
    sum_recv,
    term_send,
    term_recv,
    y_send,
    y_recv,
    x_send,
    x_recv,
):
    bands, sets, nx, pairs, slots, per_device = sizes
    ny, nz = bands // nx, sets // 2
    half = nz // 2
    stages = half // 2
    trunc = 2 * pairs * sets - 1
    group_rows = 2 * pairs
    band, group = lax.axis_index("band"), lax.axis_index("set")
    y, x = lax.div(band, nx), lax.rem(band, nx)
    z, core = lax.div(group, 2), lax.rem(group, 2)
    sibling = z * 2 + 1 - core

    def at_z(position):
        return lax.rem(position + nz, nz) * 2 + core


    def at_y(position):
        return lax.rem(position + ny, ny) * nx + x

    def at_x(position):
        return y * nx + lax.rem(position, nx)

    def needs(side, of_band):
        if side == 0:
            return slots * of_band <= trunc - pairs * group
        return slots * of_band + slots - 1 >= trunc + 1 - (pairs * group + pairs - 1)

    def row_needs(side, of_y):
        return needs(side, of_y * nx + (0 if side == 0 else nx - 1))

    peers = [(band, sibling)] + [(band, at_z(z + d)) for d in (1, -1, 2, -2)]
    if nz == 4:
        peers.pop()
    peers += [(at_y(y + d), group) for d in range(1, ny)]
    peers += [(at_x(x + d), group) for d in range(1, nx)]
    barrier = pltpu.get_barrier_semaphore()
    for peer in peers:
        pl.semaphore_signal(barrier, inc=1, device_id=peer, device_id_type=MESH)

    first = slots * band
    start = jnp.minimum(lax.div(first, 128) * 128, leg_ref.shape[2] - WINDOW)
    leg_copy = pltpu.make_async_copy(
        leg_ref.at[:, :, pl.ds(pl.multiple_of(start, 128), WINDOW)], window, leg_sem
    )
    leg_copy.start()
    rows_copy = pltpu.make_async_copy(rows_hbm, rows_ref, own_sem.at[0])
    rows_copy.start()
    grid_copy = pltpu.make_async_copy(grid_hbm, mine_raw, own_sem.at[1])
    grid_copy.start()
    folded[:, per_device:, :] = jnp.zeros_like(folded[:, per_device:, :])
    sum_in[0, 0, 0] = jnp.zeros_like(sum_in[0, 0, 0])
    sum_in[1, 0, 1] = jnp.zeros_like(sum_in[1, 0, 1])
    pl.semaphore_wait(barrier, len(peers))
    swap = pltpu.make_async_remote_copy(
        src_ref=grid_hbm,
        dst_ref=twin,
        send_sem=twin_sem.at[0],
        recv_sem=twin_sem.at[1],
        device_id=(band, sibling),
        device_id_type=MESH,
    )
    swap.start()
    rows_copy.wait()
    grid_copy.wait()

    lengths = [rows_ref[q].astype(jnp.float32) for q in range(2)]
    bases = [group * per_device, sibling * per_device]

    def prepare(source, half_index):
        for q in range(2):
            folded[q, 0:per_device, :] = source[:, q, :]
        for q in range(2):
            value = folded[q]
            point = bases[half_index] + lax.broadcasted_iota(jnp.int32, value.shape, 0)
            lane = lax.broadcasted_iota(jnp.int32, value.shape, 1)
            other = pltpu.roll(value, 64, 1)
            value = jnp.where(lane < 64, value + other, other - value)
            value = value * lax.rsqrt(jnp.full(value.shape, lengths[q], jnp.float32))
            row = lax.broadcasted_iota(jnp.int32, value.shape, 0)
            value = jnp.where((point < rows_ref[q]) & (row < per_device), value, 0.0)
            grid_high[q, half_index], grid_low[q, half_index] = split(value)

    def partials(owners):
        count = len(owners) * group_rows
        index = lax.broadcasted_iota(jnp.int32, (count, 1), 0)
        waves = jnp.zeros((count, 1), jnp.int32)
        for position, owner in enumerate(owners):
            inside = index - position * group_rows
            here = jnp.where(
                inside < pairs, pairs * owner + inside, trunc - pairs * owner - (inside - pairs)
            )
            waves = jnp.where(inside >= 0, here, waves)
        waves = waves.astype(jnp.float32)
        lane = lax.broadcasted_iota(jnp.int32, (1, 256), 1)
        results = []
        for q in range(2):
            length = jnp.full((1, 256), lengths[q], jnp.float32)
            total = jnp.zeros((2 * count, 128), jnp.float32)
            for half_index in range(2):
                points = (bases[half_index] + lane).astype(jnp.float32)
                table = jnp.concatenate(cos_sin(waves, points, length), axis=0)
                high, low = split(table)
                for factor, values in ((high, grid_high), (low, grid_high), (high, grid_low)):
                    total = total + jnp.dot(
                        factor, values[q, half_index], preferred_element_type=jnp.float32
                    )
            results.append(total)
        return results

    def sum_copy(to_right, stage, q):
        side = 0 if to_right else 1
        return pltpu.make_async_remote_copy(
            src_ref=sum_out.at[side, stage, q],
            dst_ref=sum_in.at[side, stage, q],
            send_sem=sum_send.at[side, stage, q],
            recv_sem=sum_recv.at[side, stage, q],
            device_id=(band, at_z(z + 2 if to_right else z - 2)),
            device_id_type=MESH,
        )

    def term_copy(to_right, stage):
        side = 0 if to_right else 1
        return pltpu.make_async_remote_copy(
            src_ref=term_out.at[side, stage],
            dst_ref=term_in.at[side, stage],
            send_sem=term_send.at[side, stage],
            recv_sem=term_recv.at[side, stage],
            device_id=(band, at_z(z + 1 if to_right else z - 1)),
            device_id_type=MESH,
        )

    def weights_of(pair):
        values = window[pair].astype(jnp.float32)
        values = pltpu.roll(values, lax.rem(WINDOW - (first - start), WINDOW), 1)[:, :128]
        leg_rows[...] = values
        rows = jnp.concatenate([leg_rows[pl.ds(q, bands, stride=2), :] for q in range(2)], axis=0)
        turned = jnp.transpose(rows)[: weights.shape[2]]
        turned = jnp.concatenate([turned, turned], axis=1)
        slot = first + lax.broadcasted_iota(jnp.int32, turned.shape, 0)
        parity = lax.div(lax.broadcasted_iota(jnp.int32, turned.shape, 1), 2 * bands)
        number = pairs * group + pair
        is_first = slot <= trunc - number
        even = (slot & 1) == parity
        other = ((slot - 1 - trunc + number) & 1) == parity
        weights[0, pair] = jnp.where(is_first & even, turned, 0.0).astype(jnp.bfloat16)
        weights[1, pair] = jnp.where((~is_first) & other, turned, 0.0).astype(jnp.bfloat16)

    prepare(mine_raw, 0)
    swap.wait()
    prepare(twin, 1)

    far = partials([at_z(z + half)])
    sum_out[1, 0, 0] = far[0]
    sum_copy(False, 0, 0).start()
    sum_out[0, 0, 1] = far[1]
    sum_copy(True, 0, 1).start()
    per_step = -(-pairs // max(stages - 1, 1))

    def weights_step(step):
        @pl.when(step == 1)
        def _():
            leg_copy.wait()

        def one(index, carry):
            pair = (step - 1) * per_step + index

            @pl.when(pair < pairs)
            def _():
                weights_of(pair)

            return carry

        lax.fori_loop(0, per_step, one, 0)

    def send_terms(stage):
        distance = half - 2 * stage - 1
        terms = partials([at_z(z + distance), at_z(z - distance)])
        for side in range(2):
            for q in range(2):
                for part in range(2):
                    low = (2 * part + side) * group_rows
                    term_out[side, stage, q, part * group_rows : (part + 1) * group_rows] = terms[
                        q
                    ][low : low + group_rows].astype(term_out.dtype)
            term_copy(side == 0, stage).start()

    send_terms(0)

    def stage_step(stage, carry):
        send_terms(stage)
        distance = half - 2 * stage
        mine = partials([at_z(z + distance), at_z(z - distance)])
        for side in range(2):
            term_copy(side == 0, stage - 1).wait_recv()
        for q in range(2):
            for side in range(2):
                @pl.when((stage > 1) | (q == 1 - side))
                def _():
                    sum_copy(side == 0, stage - 1, q).wait_recv()

                for part in range(2):
                    low = (2 * part + side) * group_rows
                    span = slice(part * group_rows, (part + 1) * group_rows)
                    sum_out[side, stage, q, span] = (
                        mine[q][low : low + group_rows]
                        + term_in[side, stage - 1, q, span].astype(jnp.float32)
                        + sum_in[side, stage - 1, q, span]
                    )
                sum_copy(side == 0, stage, q).start()
        weights_step(stage)
        return carry

    lax.fori_loop(1, stages, stage_step, 0)
    if stages == 1:
        weights_step(1)

    own = partials([group])
    last = stages - 1
    for side in range(2):
        term_copy(side == 0, last).wait_recv()
    for q in range(2):
        for side in range(2):
            if stages > 1 or q == 1 - side:
                sum_copy(side == 0, last, q).wait_recv()

    for q in range(2):
        total = own[q]
        for side in range(2):
            total = total + sum_in[side, last, q] + term_in[side, last, q].astype(jnp.float32)
        index = lax.broadcasted_iota(jnp.int32, (group_rows, 128), 0)
        wave = jnp.where(index < pairs, pairs * group + index, trunc - pairs * group - (index - pairs))
        usable = wave <= lax.div(rows_ref[q] - 1, 2)
        cosine = jnp.where(usable, total[:group_rows], 0.0)
        sine = jnp.where(usable, -total[group_rows:], 0.0)
        lane = lax.broadcasted_iota(jnp.int32, (group_rows, 128), 1)
        parts = (
            jnp.where(lane < 64, cosine, pltpu.roll(sine, 64, 1)),
            jnp.where(lane < 64, pltpu.roll(cosine, 64, 1), sine),
        )
        for parity in range(2):
            for side in range(2):
                at = (parity * 2 + q) * pairs
                packed[side, at : at + pairs] = parts[parity][side * pairs : (side + 1) * pairs]
    for side in range(2):
        blocks[side, band] = packed[side].astype(jnp.bfloat16)

    def y_copy(side, distance):
        return pltpu.make_async_remote_copy(
            src_ref=blocks.at[side, band],
            dst_ref=blocks.at[side, band],
            send_sem=y_send.at[side, distance],
            recv_sem=y_recv.at[side, y],
            device_id=(at_y(y + distance), group),
            device_id_type=MESH,
        )

    def y_arrival(side, source_y):
        spot = blocks.at[side, source_y * nx + x]
        return pltpu.make_async_remote_copy(
            src_ref=spot,
            dst_ref=spot,
            send_sem=y_send.at[side, 0],
            recv_sem=y_recv.at[side, source_y],
            device_id=(at_y(y + 1), group),
            device_id_type=MESH,
        )

    def x_copy(side, source_y, distance):
        spot = blocks.at[side, source_y * nx + x]
        return pltpu.make_async_remote_copy(
            src_ref=spot,
            dst_ref=spot,
            send_sem=x_send.at[side, source_y, distance],
            recv_sem=x_recv.at[side, source_y * nx + x],
            device_id=(at_x(x + distance), group),
            device_id_type=MESH,
        )

    def x_arrival(side, source):
        spot = blocks.at[side, source]
        return pltpu.make_async_remote_copy(
            src_ref=spot,
            dst_ref=spot,
            send_sem=x_send.at[side, 0, 0],
            recv_sem=x_recv.at[side, source],
            device_id=(at_x(x + 1), group),
            device_id_type=MESH,
        )

    def in_turn(index):
        step = lax.div(index + 1, 2)
        return jnp.where(lax.rem(index, 2) == 1, step, ny - step)

    def y_start(index, carry):
        distance = lax.rem(in_turn(index), ny)
        for side in range(2):
            @pl.when(row_needs(side, lax.rem(y + distance, ny)))
            def _():
                y_copy(side, distance).start()

        return carry

    lax.fori_loop(1, ny, y_start, 0)

    def unpack(side, source):
        span = 4 * pairs
        spread[side, pl.ds(pl.multiple_of(source * span, 8), span), :] = blocks[
            side, source
        ].astype(jnp.float32)

    def forward(index, carry):
        source_y = lax.rem(y + in_turn(index), ny)
        for side in range(2):
            @pl.when(row_needs(side, y) & (index > 0))
            def _():
                y_arrival(side, source_y).wait_recv()

            for distance in range(1, nx):
                @pl.when(needs(side, at_x(x + distance)))
                def _():
                    x_copy(side, source_y, distance).start()

            @pl.when(needs(side, band))
            def _():
                unpack(side, source_y * nx + x)

        return carry

    lax.fori_loop(0, ny, forward, 0)

    def collect(index, carry):
        source_y = lax.rem(y + in_turn(index), ny)
        for side in range(2):
            for distance in range(1, nx):
                @pl.when(needs(side, band))
                def _():
                    source = source_y * nx + lax.rem(x + distance, nx)
                    x_arrival(side, source).wait_recv()
                    unpack(side, source)

        return carry

    lax.fori_loop(0, ny, collect, 0)

    def legendre(sides):
        unroll = 4 if pairs % 4 == 0 else 1

        def some(index, carry):
            for step in range(unroll):
                pair = index * unroll + step
                total = None
                for side in sides:
                    parts = [
                        spread[
                            side, pl.ds((2 * parity + q) * pairs + pair, bands, stride=4 * pairs), :
                        ]
                        for parity in range(2)
                        for q in range(2)
                    ]
                    values = jnp.concatenate(parts, axis=0).astype(jnp.bfloat16)
                    result = jnp.dot(
                        weights[side, pair], values, preferred_element_type=jnp.float32
                    )[:slots]
                    total = result if total is None else total + result
                out_ref[pair] = total
            return carry

        lax.fori_loop(0, pairs // unroll, some, 0)

    pl.when(needs(0, band) & ~needs(1, band))(lambda: legendre((0,)))
    pl.when(needs(1, band) & ~needs(0, band))(lambda: legendre((1,)))
    pl.when(needs(1, band) & needs(0, band))(lambda: legendre((0, 1)))

    sum_copy(False, 0, 0).wait_send()
    sum_copy(True, 0, 1).wait_send()

    def z_sent(stage, carry):
        for side in range(2):
            term_copy(side == 0, stage).wait_send()
            for q in range(2):
                @pl.when(stage > 0)
                def _():
                    sum_copy(side == 0, stage, q).wait_send()

        return carry

    lax.fori_loop(0, stages, z_sent, 0)

    def y_sent(distance, carry):
        for side in range(2):
            @pl.when(row_needs(side, lax.rem(y + distance, ny)))
            def _():
                y_copy(side, distance).wait_send()

        return carry

    lax.fori_loop(1, ny, y_sent, 0)

    def x_sent(source_y, carry):
        for side in range(2):
            for distance in range(1, nx):
                @pl.when(needs(side, at_x(x + distance)))
                def _():
                    x_copy(side, source_y, distance).wait_send()

        return carry

    lax.fori_loop(0, ny, x_sent, 0)


def shards(nx, grid, row_points, legendre):
    bands, sets = lax.axis_size("band"), lax.axis_size("set")
    pairs, rows, width = legendre.shape
    slots = width // bands
    per_device = grid.shape[1]
    points = jnp.transpose(grid, (1, 0, 2))
    stages = sets // 8
    padded = -(-slots // 16) * 16
    group_rows = 2 * pairs
    f32, bf16 = jnp.float32, jnp.bfloat16
    sums = pltpu.VMEM((2, stages, 2, 2 * group_rows, 128), f32)
    terms = pltpu.VMEM((2, stages, 2, 2 * group_rows, 128), bf16)
    return pl.pallas_call(
        functools.partial(kernel, (bands, sets, nx, pairs, slots, per_device)),
        out_shape=jax.ShapeDtypeStruct((pairs, slots, 128), f32),
        in_specs=[
            pl.BlockSpec(memory_space=pltpu.HBM),
            pl.BlockSpec(memory_space=pltpu.HBM),
            pl.BlockSpec(memory_space=pltpu.HBM),
        ],
        out_specs=pl.BlockSpec(memory_space=pltpu.VMEM),
        scratch_shapes=[
            pltpu.SMEM((2,), jnp.int32),
            pltpu.VMEM((per_device, 2, 128), f32),
            pltpu.VMEM((per_device, 2, 128), f32),
            pltpu.VMEM((2, 256, 128), f32),
            pltpu.VMEM((2, 2, 256, 128), bf16),
            pltpu.VMEM((2, 2, 256, 128), bf16),
            pltpu.VMEM((pairs, rows, WINDOW), bf16),
            pltpu.VMEM((rows, 128), f32),
            pltpu.VMEM((2, pairs, padded, 2 * rows), bf16),
            sums,
            sums,
            terms,
            terms,
            pltpu.VMEM((2, 4 * pairs, 128), f32),
            pltpu.VMEM((2, bands, 4 * pairs, 128), bf16),
            pltpu.VMEM((2, bands * 4 * pairs, 128), f32),
            pltpu.SemaphoreType.DMA,
            pltpu.SemaphoreType.DMA((2,)),
            pltpu.SemaphoreType.DMA((2,)),
            pltpu.SemaphoreType.DMA((2, stages, 2)),
            pltpu.SemaphoreType.DMA((2, stages, 2)),
            pltpu.SemaphoreType.DMA((2, stages)),
            pltpu.SemaphoreType.DMA((2, stages)),
            pltpu.SemaphoreType.DMA((2, bands // nx)),
            pltpu.SemaphoreType.DMA((2, bands // nx)),
            pltpu.SemaphoreType.DMA((2, bands // nx, nx)),
            pltpu.SemaphoreType.DMA((2, bands)),
        ],
        compiler_params=pltpu.CompilerParams(
            collective_id=0, has_side_effects=True, vmem_limit_bytes=62900000
        ),
    )(row_points, points, legendre)


def solution(mesh, nx=CHIPS_X):
    return jax.shard_map(
        functools.partial(shards, nx),
        mesh=mesh,
        in_specs=(P("band", "set", None), P("band"), P("set", None, None)),
        out_specs=P("set", "band", None),
        check_vma=False,
    )
```

```python
import functools
import math

import jax
import jax.numpy as jnp
from jax import lax
from jax.experimental import pallas as pl
from jax.experimental.pallas import tpu as pltpu
from jax.sharding import PartitionSpec as P

MESH = pl.DeviceIdType.MESH
CHIPS_X = 4
WINDOW = 256
SIN_TERMS = (1.0, -1 / 6, 1 / 120, -1 / 5040, 1 / 362880, -1 / 39916800)
COS_TERMS = (1.0, -1 / 2, 1 / 24, -1 / 720, 1 / 40320, -1 / 3628800, 1 / 479001600)


def horner(terms, square):
    total = jnp.full_like(square, terms[-1])
    for term in terms[-2::-1]:
        total = total * square + term
    return total


def cos_sin(waves, points, length):
    product = waves * points
    residue = product - jnp.floor(product * (1.0 / length) + 0.5) * length
    half = residue * (math.pi / length)
    square = half * half
    sine = half * horner(SIN_TERMS, square)
    cosine = horner(COS_TERMS, square)
    return 1.0 - 2.0 * sine * sine, 2.0 * sine * cosine


def split(value):
    high = value.astype(jnp.bfloat16)
    return high, (value - high.astype(jnp.float32)).astype(jnp.bfloat16)


def kernel(
    sizes,
    rows_hbm,
    grid_hbm,
    leg_ref,
    out_ref,
    rows_ref,
    mine_raw,
    twin,
    folded,
    grid_high,
    grid_low,
    window,
    leg_rows,
    weights,
    base_cos,
    base_sin,
    early_out,
    early_in,
    sum_out,
    sum_in,
    term_out,
    term_in,
    packed,
    blocks,
    spread,
    leg_sem,
    own_sem,
    twin_sem,
    sum_send,
    sum_recv,
    term_send,
    term_recv,
    y_send,
    y_recv,
    x_send,
    x_recv,
):
    bands, sets, nx, pairs, slots, per_device = sizes
    ny, nz = bands // nx, sets // 2
    half = nz // 2
    stages = half // 2
    early = early_in.shape[1]
    trunc = 2 * pairs * sets - 1
    group_rows = 2 * pairs
    band, group = lax.axis_index("band"), lax.axis_index("set")
    y, x = lax.div(band, nx), lax.rem(band, nx)
    z, core = lax.div(group, 2), lax.rem(group, 2)
    sibling = z * 2 + 1 - core

    def at_z(position):
        return lax.rem(position + nz, nz) * 2 + core


    def at_y(position):
        return lax.rem(position + ny, ny) * nx + x

    def at_x(position):
        return y * nx + lax.rem(position, nx)

    def needs(side, of_band):
        if side == 0:
            return slots * of_band <= trunc - pairs * group
        return slots * of_band + slots - 1 >= trunc + 1 - (pairs * group + pairs - 1)

    def row_needs(side, of_y):
        return needs(side, of_y * nx + (0 if side == 0 else nx - 1))

    peers = [(band, sibling)] + [(band, at_z(z + d)) for d in (1, -1, 2, -2)]
    if nz == 4:
        peers.pop()
    peers += [(at_y(y + d), group) for d in range(1, ny)]
    peers += [(at_x(x + d), group) for d in range(1, nx)]
    barrier = pltpu.get_barrier_semaphore()
    for peer in peers:
        pl.semaphore_signal(barrier, inc=1, device_id=peer, device_id_type=MESH)

    first = slots * band
    start = jnp.minimum(lax.div(first, 128) * 128, leg_ref.shape[2] - WINDOW)
    leg_copy = pltpu.make_async_copy(
        leg_ref.at[:, :, pl.ds(pl.multiple_of(start, 128), WINDOW)], window, leg_sem
    )
    leg_copy.start()
    rows_copy = pltpu.make_async_copy(rows_hbm, rows_ref, own_sem.at[0])
    rows_copy.start()
    grid_copy = pltpu.make_async_copy(grid_hbm, mine_raw, own_sem.at[1])
    grid_copy.start()
    folded[:, per_device:, :] = jnp.zeros_like(folded[:, per_device:, :])
    swap = pltpu.make_async_remote_copy(
        src_ref=grid_hbm,
        dst_ref=twin,
        send_sem=twin_sem.at[0],
        recv_sem=twin_sem.at[1],
        device_id=(band, sibling),
        device_id_type=MESH,
    )
    rows_copy.wait()
    lengths = [rows_ref[q].astype(jnp.float32) for q in range(2)]
    bases = [group * per_device, sibling * per_device]

    def prepare(source, half_index):
        for q in range(2):
            folded[q, 0:per_device, :] = source[:, q, :]
        for q in range(2):
            value = folded[q]
            point = bases[half_index] + lax.broadcasted_iota(jnp.int32, value.shape, 0)
            lane = lax.broadcasted_iota(jnp.int32, value.shape, 1)
            other = pltpu.roll(value, 64, 1)
            value = jnp.where(lane < 64, value + other, other - value)
            value = value * lax.rsqrt(jnp.full(value.shape, lengths[q], jnp.float32))
            row = lax.broadcasted_iota(jnp.int32, value.shape, 0)
            value = jnp.where((point < rows_ref[q]) & (row < per_device), value, 0.0)
            grid_high[q, half_index], grid_low[q, half_index] = split(value)

    def base_tables():
        index = lax.broadcasted_iota(jnp.int32, (group_rows, 256), 0)
        waves = jnp.where(index < pairs, index, trunc - (index - pairs)).astype(jnp.float32)
        lane = lax.broadcasted_iota(jnp.int32, (group_rows, 256), 1)
        for q in range(2):
            length = jnp.full((group_rows, 256), lengths[q], jnp.float32)
            for half_index in range(2):
                points = (bases[half_index] + lane).astype(jnp.float32)
                cosine, sine = cos_sin(waves, points, length)
                base_cos[q, half_index] = cosine
                base_sin[q, half_index] = sine

    def partials(owners):
        count = len(owners) * group_rows
        lane = lax.broadcasted_iota(jnp.int32, (8, 256), 1)
        upward = lax.broadcasted_iota(jnp.int32, (group_rows, 256), 0) < pairs
        results = []
        for q in range(2):
            length = jnp.full((8, 256), lengths[q], jnp.float32)
            total = jnp.zeros((2 * count, 128), jnp.float32)
            for half_index in range(2):
                points = (bases[half_index] + lane).astype(jnp.float32)
                cosine, sine = base_cos[q, half_index], base_sin[q, half_index]
                cosines, sines = [], []
                for owner in owners:
                    waves = jnp.full((8, 256), pairs * owner, jnp.int32).astype(jnp.float32)
                    turn_cos, turn_sin = (
                        jnp.concatenate([part] * (group_rows // 8), axis=0)
                        for part in cos_sin(waves, points, length)
                    )
                    turn_sin = jnp.where(upward, turn_sin, -turn_sin)
                    cosines.append(cosine * turn_cos - sine * turn_sin)
                    sines.append(sine * turn_cos + cosine * turn_sin)
                high, low = split(jnp.concatenate(cosines + sines, axis=0))
                for factor, values in ((high, grid_high), (low, grid_high), (high, grid_low)):
                    total = total + jnp.dot(
                        factor, values[q, half_index], preferred_element_type=jnp.float32
                    )
            results.append(total)
        return results

    def sum_slots(stage):
        return (early_out, early_in, stage) if stage < early else (sum_out, sum_in, stage - early)

    def sum_copy(to_right, stage, q):
        side = 0 if to_right else 1
        source, target, slot = sum_slots(stage)
        return pltpu.make_async_remote_copy(
            src_ref=source.at[side, slot, q],
            dst_ref=target.at[side, slot, q],
            send_sem=sum_send.at[side, stage, q],
            recv_sem=sum_recv.at[side, stage, q],
            device_id=(band, at_z(z + 2 if to_right else z - 2)),
            device_id_type=MESH,
        )

    def term_copy(to_right, stage):
        side = 0 if to_right else 1
        return pltpu.make_async_remote_copy(
            src_ref=term_out.at[side, stage],
            dst_ref=term_in.at[side, stage],
            send_sem=term_send.at[side, stage],
            recv_sem=term_recv.at[side, stage],
            device_id=(band, at_z(z + 1 if to_right else z - 1)),
            device_id_type=MESH,
        )

    def weights_of(pair):
        values = window[pair].astype(jnp.float32)
        values = pltpu.roll(values, lax.rem(WINDOW - (first - start), WINDOW), 1)[:, :128]
        leg_rows[...] = values
        rows = jnp.concatenate([leg_rows[pl.ds(q, bands, stride=2), :] for q in range(2)], axis=0)
        turned = jnp.transpose(rows)[: weights.shape[2]]
        turned = jnp.concatenate([turned, turned], axis=1)
        slot = first + lax.broadcasted_iota(jnp.int32, turned.shape, 0)
        parity = lax.div(lax.broadcasted_iota(jnp.int32, turned.shape, 1), 2 * bands)
        number = pairs * group + pair
        is_first = slot <= trunc - number
        even = (slot & 1) == parity
        other = ((slot - 1 - trunc + number) & 1) == parity
        weights[0, pair] = jnp.where(is_first & even, turned, 0.0).astype(jnp.bfloat16)
        weights[1, pair] = jnp.where((~is_first) & other, turned, 0.0).astype(jnp.bfloat16)

    base_tables()
    pl.semaphore_wait(barrier, len(peers))
    swap.start()
    grid_copy.wait()
    prepare(mine_raw, 0)
    swap.wait()
    prepare(twin, 1)

    far = partials([at_z(z + half)])
    first_out = sum_slots(0)[0]
    first_out[1, 0, 0] = far[0].astype(first_out.dtype)
    sum_copy(False, 0, 0).start()
    first_out[0, 0, 1] = far[1].astype(first_out.dtype)
    sum_copy(True, 0, 1).start()
    per_step = -(-pairs // max(stages - 1, 1))

    def weights_step(step):
        if step == 1:
            leg_copy.wait()

        def one(index, carry):
            pair = (step - 1) * per_step + index

            @pl.when(pair < pairs)
            def _():
                weights_of(pair)

            return carry

        lax.fori_loop(0, per_step, one, 0)

    def send_terms(stage):
        distance = half - 2 * stage - 1
        terms = partials([at_z(z + distance), at_z(z - distance)])
        for side in range(2):
            for q in range(2):
                for part in range(2):
                    low = (2 * part + side) * group_rows
                    term_out[side, stage, q, part * group_rows : (part + 1) * group_rows] = terms[
                        q
                    ][low : low + group_rows].astype(term_out.dtype)
            term_copy(side == 0, stage).start()

    send_terms(0)

    for stage in range(1, stages):
        send_terms(stage)
        distance = half - 2 * stage
        mine = partials([at_z(z + distance), at_z(z - distance)])
        for side in range(2):
            term_copy(side == 0, stage - 1).wait_recv()
        source, _, slot = sum_slots(stage)
        _, came, came_slot = sum_slots(stage - 1)
        for q in range(2):
            for side in range(2):
                has_sum = stage > 1 or q == 1 - side
                if has_sum:
                    sum_copy(side == 0, stage - 1, q).wait_recv()
                for part in range(2):
                    low = (2 * part + side) * group_rows
                    span = slice(part * group_rows, (part + 1) * group_rows)
                    total = mine[q][low : low + group_rows]
                    total = total + term_in[side, stage - 1, q, span].astype(jnp.float32)
                    if has_sum:
                        total = total + came[side, came_slot, q, span].astype(jnp.float32)
                    source[side, slot, q, span] = total.astype(source.dtype)
                sum_copy(side == 0, stage, q).start()
        weights_step(stage)
    if stages == 1:
        weights_step(1)

    own = partials([group])
    last = stages - 1
    for side in range(2):
        term_copy(side == 0, last).wait_recv()
    for q in range(2):
        for side in range(2):
            if stages > 1 or q == 1 - side:
                sum_copy(side == 0, last, q).wait_recv()

    for q in range(2):
        total = own[q]
        _, came, slot = sum_slots(last)
        for side in range(2):
            total = total + term_in[side, last, q].astype(jnp.float32)
            if stages > 1 or q == 1 - side:
                total = total + came[side, slot, q].astype(jnp.float32)
        index = lax.broadcasted_iota(jnp.int32, (group_rows, 128), 0)
        wave = jnp.where(index < pairs, pairs * group + index, trunc - pairs * group - (index - pairs))
        usable = wave <= lax.div(rows_ref[q] - 1, 2)
        cosine = jnp.where(usable, total[:group_rows], 0.0)
        sine = jnp.where(usable, -total[group_rows:], 0.0)
        lane = lax.broadcasted_iota(jnp.int32, (group_rows, 128), 1)
        parts = (
            jnp.where(lane < 64, cosine, pltpu.roll(sine, 64, 1)),
            jnp.where(lane < 64, pltpu.roll(cosine, 64, 1), sine),
        )
        for parity in range(2):
            for side in range(2):
                at = (parity * 2 + q) * pairs
                packed[side, at : at + pairs] = parts[parity][side * pairs : (side + 1) * pairs]
    for side in range(2):
        blocks[side, band] = packed[side].astype(jnp.bfloat16)

    def y_copy(side, distance):
        return pltpu.make_async_remote_copy(
            src_ref=blocks.at[side, band],
            dst_ref=blocks.at[side, band],
            send_sem=y_send.at[side, distance],
            recv_sem=y_recv.at[side, y],
            device_id=(at_y(y + distance), group),
            device_id_type=MESH,
        )

    def y_arrival(side, source_y):
        spot = blocks.at[side, source_y * nx + x]
        return pltpu.make_async_remote_copy(
            src_ref=spot,
            dst_ref=spot,
            send_sem=y_send.at[side, 0],
            recv_sem=y_recv.at[side, source_y],
            device_id=(at_y(y + 1), group),
            device_id_type=MESH,
        )

    def x_copy(side, source_y, distance):
        spot = blocks.at[side, source_y * nx + x]
        return pltpu.make_async_remote_copy(
            src_ref=spot,
            dst_ref=spot,
            send_sem=x_send.at[side, source_y, distance],
            recv_sem=x_recv.at[side, source_y * nx + x],
            device_id=(at_x(x + distance), group),
            device_id_type=MESH,
        )

    def x_arrival(side, source):
        spot = blocks.at[side, source]
        return pltpu.make_async_remote_copy(
            src_ref=spot,
            dst_ref=spot,
            send_sem=x_send.at[side, 0, 0],
            recv_sem=x_recv.at[side, source],
            device_id=(at_x(x + 1), group),
            device_id_type=MESH,
        )

    def in_turn(index):
        step = lax.div(index + 1, 2)
        return jnp.where(lax.rem(index, 2) == 1, step, ny - step)

    def y_start(index, carry):
        distance = lax.rem(in_turn(index), ny)
        for side in range(2):
            @pl.when(row_needs(side, lax.rem(y + distance, ny)))
            def _():
                y_copy(side, distance).start()

        return carry

    lax.fori_loop(1, ny, y_start, 0)

    def unpack(side, source):
        span = 4 * pairs
        spread[side, pl.ds(pl.multiple_of(source * span, 8), span), :] = blocks[
            side, source
        ].astype(jnp.float32)

    def forward(index, carry):
        source_y = lax.rem(y + in_turn(index), ny)
        for side in range(2):
            @pl.when(row_needs(side, y) & (index > 0))
            def _():
                y_arrival(side, source_y).wait_recv()

            for distance in range(1, nx):
                @pl.when(needs(side, at_x(x + distance)))
                def _():
                    x_copy(side, source_y, distance).start()

            @pl.when(needs(side, band))
            def _():
                unpack(side, source_y * nx + x)

        return carry

    lax.fori_loop(0, ny, forward, 0)

    def collect(index, carry):
        source_y = lax.rem(y + in_turn(index), ny)
        for side in range(2):
            for distance in range(1, nx):
                @pl.when(needs(side, band))
                def _():
                    source = source_y * nx + lax.rem(x + distance, nx)
                    x_arrival(side, source).wait_recv()
                    unpack(side, source)

        return carry

    lax.fori_loop(0, ny, collect, 0)

    def legendre(sides):
        unroll = 4 if pairs % 4 == 0 else 1

        def some(index, carry):
            for step in range(unroll):
                pair = index * unroll + step
                total = None
                for side in sides:
                    parts = [
                        spread[
                            side, pl.ds((2 * parity + q) * pairs + pair, bands, stride=4 * pairs), :
                        ]
                        for parity in range(2)
                        for q in range(2)
                    ]
                    values = jnp.concatenate(parts, axis=0).astype(jnp.bfloat16)
                    result = jnp.dot(
                        weights[side, pair], values, preferred_element_type=jnp.float32
                    )[:slots]
                    total = result if total is None else total + result
                out_ref[pair] = total
            return carry

        lax.fori_loop(0, pairs // unroll, some, 0)

    pl.when(needs(0, band) & ~needs(1, band))(lambda: legendre((0,)))
    pl.when(needs(1, band) & ~needs(0, band))(lambda: legendre((1,)))
    pl.when(needs(1, band) & needs(0, band))(lambda: legendre((0, 1)))

    sum_copy(False, 0, 0).wait_send()
    sum_copy(True, 0, 1).wait_send()

    for stage in range(stages):
        for side in range(2):
            term_copy(side == 0, stage).wait_send()
            for q in range(2):
                if stage:
                    sum_copy(side == 0, stage, q).wait_send()

    def y_sent(distance, carry):
        for side in range(2):
            @pl.when(row_needs(side, lax.rem(y + distance, ny)))
            def _():
                y_copy(side, distance).wait_send()

        return carry

    lax.fori_loop(1, ny, y_sent, 0)

    def x_sent(source_y, carry):
        for side in range(2):
            for distance in range(1, nx):
                @pl.when(needs(side, at_x(x + distance)))
                def _():
                    x_copy(side, source_y, distance).wait_send()

        return carry

    lax.fori_loop(0, ny, x_sent, 0)


def shards(nx, grid, row_points, legendre):
    bands, sets = lax.axis_size("band"), lax.axis_size("set")
    pairs, rows, width = legendre.shape
    slots = width // bands
    per_device = grid.shape[1]
    points = jnp.transpose(grid, (1, 0, 2))
    stages = sets // 8
    padded = -(-slots // 16) * 16
    group_rows = 2 * pairs
    f32, bf16 = jnp.float32, jnp.bfloat16
    table = pltpu.VMEM((2, 2, group_rows, 256), f32)
    early = min(2, stages)
    early_sums = pltpu.VMEM((2, early, 2, 2 * group_rows, 128), bf16)
    sums = pltpu.VMEM((2, max(stages - early, 1), 2, 2 * group_rows, 128), f32)
    terms = pltpu.VMEM((2, stages, 2, 2 * group_rows, 128), bf16)
    return pl.pallas_call(
        functools.partial(kernel, (bands, sets, nx, pairs, slots, per_device)),
        out_shape=jax.ShapeDtypeStruct((pairs, slots, 128), f32),
        in_specs=[
            pl.BlockSpec(memory_space=pltpu.HBM),
            pl.BlockSpec(memory_space=pltpu.HBM),
            pl.BlockSpec(memory_space=pltpu.HBM),
        ],
        out_specs=pl.BlockSpec(memory_space=pltpu.VMEM),
        scratch_shapes=[
            pltpu.SMEM((2,), jnp.int32),
            pltpu.VMEM((per_device, 2, 128), f32),
            pltpu.VMEM((per_device, 2, 128), f32),
            pltpu.VMEM((2, 256, 128), f32),
            pltpu.VMEM((2, 2, 256, 128), bf16),
            pltpu.VMEM((2, 2, 256, 128), bf16),
            pltpu.VMEM((pairs, rows, WINDOW), bf16),
            pltpu.VMEM((rows, 128), f32),
            pltpu.VMEM((2, pairs, padded, 2 * rows), bf16),
            table,
            table,
            early_sums,
            early_sums,
            sums,
            sums,
            terms,
            terms,
            pltpu.VMEM((2, 4 * pairs, 128), f32),
            pltpu.VMEM((2, bands, 4 * pairs, 128), bf16),
            pltpu.VMEM((2, bands * 4 * pairs, 128), f32),
            pltpu.SemaphoreType.DMA,
            pltpu.SemaphoreType.DMA((2,)),
            pltpu.SemaphoreType.DMA((2,)),
            pltpu.SemaphoreType.DMA((2, stages, 2)),
            pltpu.SemaphoreType.DMA((2, stages, 2)),
            pltpu.SemaphoreType.DMA((2, stages)),
            pltpu.SemaphoreType.DMA((2, stages)),
            pltpu.SemaphoreType.DMA((2, bands // nx)),
            pltpu.SemaphoreType.DMA((2, bands // nx)),
            pltpu.SemaphoreType.DMA((2, bands // nx, nx)),
            pltpu.SemaphoreType.DMA((2, bands)),
        ],
        compiler_params=pltpu.CompilerParams(
            collective_id=0, has_side_effects=True, vmem_limit_bytes=62900000
        ),
    )(row_points, points, legendre)


def solution(mesh, nx=CHIPS_X):
    return jax.shard_map(
        functools.partial(shards, nx),
        mesh=mesh,
        in_specs=(P("band", "set", None), P("band"), P("set", None, None)),
        out_specs=P("set", "band", None),
        check_vma=False,
    )
```

```python
import functools
import math

import jax
import jax.numpy as jnp
from jax import lax
from jax.experimental import pallas as pl
from jax.experimental.pallas import tpu as pltpu
from jax.sharding import PartitionSpec as P

MESH = pl.DeviceIdType.MESH
CHIPS_X = 4
WINDOW = 256
SIN_TERMS = (1.0, -1 / 6, 1 / 120, -1 / 5040, 1 / 362880, -1 / 39916800)
COS_TERMS = (1.0, -1 / 2, 1 / 24, -1 / 720, 1 / 40320, -1 / 3628800, 1 / 479001600)


def horner(terms, square):
    total = jnp.full_like(square, terms[-1])
    for term in terms[-2::-1]:
        total = total * square + term
    return total


def cos_sin(waves, points, length):
    product = waves * points
    residue = product - jnp.floor(product * (1.0 / length) + 0.5) * length
    half = residue * (math.pi / length)
    square = half * half
    sine = half * horner(SIN_TERMS, square)
    cosine = horner(COS_TERMS, square)
    return 1.0 - 2.0 * sine * sine, 2.0 * sine * cosine


def split(value):
    high = value.astype(jnp.bfloat16)
    return high, (value - high.astype(jnp.float32)).astype(jnp.bfloat16)


def kernel(
    sizes,
    rows_hbm,
    grid_hbm,
    leg_ref,
    out_ref,
    rows_ref,
    mine_raw,
    twin,
    folded,
    grid_high,
    grid_low,
    window,
    leg_rows,
    weights,
    base_cos,
    base_sin,
    early_out,
    early_in,
    sum_out,
    sum_in,
    term_out,
    term_in,
    packed,
    blocks,
    spread,
    leg_sem,
    own_sem,
    twin_sem,
    sum_send,
    sum_recv,
    term_send,
    term_recv,
    y_send,
    y_recv,
    x_send,
    x_recv,
):
    bands, sets, nx, pairs, slots, per_device = sizes
    ny, nz = bands // nx, sets // 2
    half = nz // 2
    stages = half // 2
    early = early_in.shape[1]
    trunc = 2 * pairs * sets - 1
    group_rows = 2 * pairs
    band, group = lax.axis_index("band"), lax.axis_index("set")
    y, x = lax.div(band, nx), lax.rem(band, nx)
    z, core = lax.div(group, 2), lax.rem(group, 2)
    sibling = z * 2 + 1 - core

    def at_z(position):
        return lax.rem(position + nz, nz) * 2 + core


    def at_y(position):
        return lax.rem(position + ny, ny) * nx + x

    def at_x(position):
        return y * nx + lax.rem(position, nx)

    def needs(side, of_band):
        if side == 0:
            return slots * of_band <= trunc - pairs * group
        return slots * of_band + slots - 1 >= trunc + 1 - (pairs * group + pairs - 1)

    def row_needs(side, of_y):
        return needs(side, of_y * nx + (0 if side == 0 else nx - 1))

    stride = (trunc + 1) // (2 * bands)

    def holds(side, of_band):
        lowest = pairs * group if side == 0 else trunc - pairs * group - (pairs - 1)
        return lowest <= 4 * stride * (of_band + 1) + 7

    peers = [(band, sibling)] + [(band, at_z(z + d)) for d in (1, -1, 2, -2)]
    if nz == 4:
        peers.pop()
    peers += [(at_y(y + d), group) for d in range(1, ny)]
    peers += [(at_x(x + d), group) for d in range(1, nx)]
    barrier = pltpu.get_barrier_semaphore()
    for peer in peers:
        pl.semaphore_signal(barrier, inc=1, device_id=peer, device_id_type=MESH)

    first = slots * band
    start = jnp.minimum(lax.div(first, 128) * 128, leg_ref.shape[2] - WINDOW)
    leg_copy = pltpu.make_async_copy(
        leg_ref.at[:, :, pl.ds(pl.multiple_of(start, 128), WINDOW)], window, leg_sem
    )
    leg_copy.start()
    rows_copy = pltpu.make_async_copy(rows_hbm, rows_ref, own_sem.at[0])
    rows_copy.start()
    grid_copy = pltpu.make_async_copy(grid_hbm, mine_raw, own_sem.at[1])
    grid_copy.start()
    folded[:, per_device:, :] = jnp.zeros_like(folded[:, per_device:, :])
    swap = pltpu.make_async_remote_copy(
        src_ref=grid_hbm,
        dst_ref=twin,
        send_sem=twin_sem.at[0],
        recv_sem=twin_sem.at[1],
        device_id=(band, sibling),
        device_id_type=MESH,
    )
    rows_copy.wait()
    lengths = [rows_ref[q].astype(jnp.float32) for q in range(2)]
    bases = [group * per_device, sibling * per_device]

    def prepare(source, half_index):
        for q in range(2):
            folded[q, 0:per_device, :] = source[:, q, :]
        for q in range(2):
            value = folded[q]
            point = bases[half_index] + lax.broadcasted_iota(jnp.int32, value.shape, 0)
            lane = lax.broadcasted_iota(jnp.int32, value.shape, 1)
            other = pltpu.roll(value, 64, 1)
            value = jnp.where(lane < 64, value + other, other - value)
            value = value * lax.rsqrt(jnp.full(value.shape, lengths[q], jnp.float32))
            row = lax.broadcasted_iota(jnp.int32, value.shape, 0)
            value = jnp.where((point < rows_ref[q]) & (row < per_device), value, 0.0)
            grid_high[q, half_index], grid_low[q, half_index] = split(value)

    def base_tables():
        index = lax.broadcasted_iota(jnp.int32, (group_rows, 256), 0)
        waves = jnp.where(index < pairs, index, trunc - (index - pairs)).astype(jnp.float32)
        lane = lax.broadcasted_iota(jnp.int32, (group_rows, 256), 1)
        for q in range(2):
            length = jnp.full((group_rows, 256), lengths[q], jnp.float32)
            for half_index in range(2):
                points = (bases[half_index] + lane).astype(jnp.float32)
                cosine, sine = cos_sin(waves, points, length)
                base_cos[q, half_index] = cosine
                base_sin[q, half_index] = sine

    def partials(owners):
        count = len(owners) * group_rows
        lane = lax.broadcasted_iota(jnp.int32, (8, 256), 1)
        upward = lax.broadcasted_iota(jnp.int32, (group_rows, 256), 0) < pairs
        results = []
        for q in range(2):
            length = jnp.full((8, 256), lengths[q], jnp.float32)
            total = jnp.zeros((2 * count, 128), jnp.float32)
            for half_index in range(2):
                points = (bases[half_index] + lane).astype(jnp.float32)
                cosine, sine = base_cos[q, half_index], base_sin[q, half_index]
                cosines, sines = [], []
                for owner in owners:
                    waves = jnp.full((8, 256), pairs * owner, jnp.int32).astype(jnp.float32)
                    turn_cos, turn_sin = (
                        jnp.concatenate([part] * (group_rows // 8), axis=0)
                        for part in cos_sin(waves, points, length)
                    )
                    turn_sin = jnp.where(upward, turn_sin, -turn_sin)
                    cosines.append(cosine * turn_cos - sine * turn_sin)
                    sines.append(sine * turn_cos + cosine * turn_sin)
                high, low = split(jnp.concatenate(cosines + sines, axis=0))
                for factor, values in ((high, grid_high), (low, grid_high), (high, grid_low)):
                    total = total + jnp.dot(
                        factor, values[q, half_index], preferred_element_type=jnp.float32
                    )
            results.append(total)
        return results

    def sum_slots(stage):
        return (early_out, early_in, stage) if stage < early else (sum_out, sum_in, stage - early)

    def sum_copy(to_right, stage, q):
        side = 0 if to_right else 1
        source, target, slot = sum_slots(stage)
        return pltpu.make_async_remote_copy(
            src_ref=source.at[side, slot, q],
            dst_ref=target.at[side, slot, q],
            send_sem=sum_send.at[side, stage, q],
            recv_sem=sum_recv.at[side, stage, q],
            device_id=(band, at_z(z + 2 if to_right else z - 2)),
            device_id_type=MESH,
        )

    def term_copy(to_right, stage):
        side = 0 if to_right else 1
        return pltpu.make_async_remote_copy(
            src_ref=term_out.at[side, stage],
            dst_ref=term_in.at[side, stage],
            send_sem=term_send.at[side, stage],
            recv_sem=term_recv.at[side, stage],
            device_id=(band, at_z(z + 1 if to_right else z - 1)),
            device_id_type=MESH,
        )

    def weights_of(pair):
        values = window[pair].astype(jnp.float32)
        values = pltpu.roll(values, lax.rem(WINDOW - (first - start), WINDOW), 1)[:, :128]
        leg_rows[...] = values
        rows = jnp.concatenate([leg_rows[pl.ds(q, bands, stride=2), :] for q in range(2)], axis=0)
        turned = jnp.transpose(rows)[: weights.shape[2]]
        turned = jnp.concatenate([turned, turned], axis=1)
        slot = first + lax.broadcasted_iota(jnp.int32, turned.shape, 0)
        parity = lax.div(lax.broadcasted_iota(jnp.int32, turned.shape, 1), 2 * bands)
        number = pairs * group + pair
        is_first = slot <= trunc - number
        even = (slot & 1) == parity
        other = ((slot - 1 - trunc + number) & 1) == parity
        weights[0, pair] = jnp.where(is_first & even, turned, 0.0).astype(jnp.bfloat16)
        weights[1, pair] = jnp.where((~is_first) & other, turned, 0.0).astype(jnp.bfloat16)

    base_tables()
    pl.semaphore_wait(barrier, len(peers))
    swap.start()
    grid_copy.wait()
    prepare(mine_raw, 0)
    swap.wait()
    prepare(twin, 1)

    far = partials([at_z(z + half)])
    first_out = sum_slots(0)[0]
    first_out[1, 0, 0] = far[0].astype(first_out.dtype)
    sum_copy(False, 0, 0).start()
    first_out[0, 0, 1] = far[1].astype(first_out.dtype)
    sum_copy(True, 0, 1).start()
    per_step = -(-pairs // max(stages - 1, 1))

    def weights_step(step):
        if step == 1:
            leg_copy.wait()
            spread[...] = jnp.zeros_like(spread)

        def one(index, carry):
            pair = (step - 1) * per_step + index

            @pl.when(pair < pairs)
            def _():
                weights_of(pair)

            return carry

        lax.fori_loop(0, per_step, one, 0)

    def send_terms(stage):
        distance = half - 2 * stage - 1
        terms = partials([at_z(z + distance), at_z(z - distance)])
        for side in range(2):
            for q in range(2):
                for part in range(2):
                    low = (2 * part + side) * group_rows
                    term_out[side, stage, q, part * group_rows : (part + 1) * group_rows] = terms[
                        q
                    ][low : low + group_rows].astype(term_out.dtype)
            term_copy(side == 0, stage).start()

    send_terms(0)

    for stage in range(1, stages):
        send_terms(stage)
        distance = half - 2 * stage
        mine = partials([at_z(z + distance), at_z(z - distance)])
        for side in range(2):
            term_copy(side == 0, stage - 1).wait_recv()
        source, _, slot = sum_slots(stage)
        _, came, came_slot = sum_slots(stage - 1)
        for q in range(2):
            for side in range(2):
                has_sum = stage > 1 or q == 1 - side
                if has_sum:
                    sum_copy(side == 0, stage - 1, q).wait_recv()
                for part in range(2):
                    low = (2 * part + side) * group_rows
                    span = slice(part * group_rows, (part + 1) * group_rows)
                    total = mine[q][low : low + group_rows]
                    total = total + term_in[side, stage - 1, q, span].astype(jnp.float32)
                    if has_sum:
                        total = total + came[side, came_slot, q, span].astype(jnp.float32)
                    source[side, slot, q, span] = total.astype(source.dtype)
                sum_copy(side == 0, stage, q).start()
        weights_step(stage)
    if stages == 1:
        weights_step(1)

    own = partials([group])
    last = stages - 1
    for side in range(2):
        term_copy(side == 0, last).wait_recv()
    for q in range(2):
        for side in range(2):
            if stages > 1 or q == 1 - side:
                sum_copy(side == 0, last, q).wait_recv()

    for q in range(2):
        total = own[q]
        _, came, slot = sum_slots(last)
        for side in range(2):
            total = total + term_in[side, last, q].astype(jnp.float32)
            if stages > 1 or q == 1 - side:
                total = total + came[side, slot, q].astype(jnp.float32)
        index = lax.broadcasted_iota(jnp.int32, (group_rows, 128), 0)
        wave = jnp.where(index < pairs, pairs * group + index, trunc - pairs * group - (index - pairs))
        usable = wave <= lax.div(rows_ref[q] - 1, 2)
        cosine = jnp.where(usable, total[:group_rows], 0.0)
        sine = jnp.where(usable, -total[group_rows:], 0.0)
        lane = lax.broadcasted_iota(jnp.int32, (group_rows, 128), 1)
        parts = (
            jnp.where(lane < 64, cosine, pltpu.roll(sine, 64, 1)),
            jnp.where(lane < 64, pltpu.roll(cosine, 64, 1), sine),
        )
        for parity in range(2):
            for side in range(2):
                at = (parity * 2 + q) * pairs
                packed[side, at : at + pairs] = parts[parity][side * pairs : (side + 1) * pairs]
    for side in range(2):
        blocks[side, band] = packed[side].astype(jnp.bfloat16)

    def y_copy(side, distance):
        return pltpu.make_async_remote_copy(
            src_ref=blocks.at[side, band],
            dst_ref=blocks.at[side, band],
            send_sem=y_send.at[side, distance],
            recv_sem=y_recv.at[side, y],
            device_id=(at_y(y + distance), group),
            device_id_type=MESH,
        )

    def y_arrival(side, source_y):
        spot = blocks.at[side, source_y * nx + x]
        return pltpu.make_async_remote_copy(
            src_ref=spot,
            dst_ref=spot,
            send_sem=y_send.at[side, 0],
            recv_sem=y_recv.at[side, source_y],
            device_id=(at_y(y + 1), group),
            device_id_type=MESH,
        )

    def x_copy(side, source_y, distance):
        spot = blocks.at[side, source_y * nx + x]
        return pltpu.make_async_remote_copy(
            src_ref=spot,
            dst_ref=spot,
            send_sem=x_send.at[side, source_y, distance],
            recv_sem=x_recv.at[side, source_y * nx + x],
            device_id=(at_x(x + distance), group),
            device_id_type=MESH,
        )

    def x_arrival(side, source):
        spot = blocks.at[side, source]
        return pltpu.make_async_remote_copy(
            src_ref=spot,
            dst_ref=spot,
            send_sem=x_send.at[side, 0, 0],
            recv_sem=x_recv.at[side, source],
            device_id=(at_x(x + 1), group),
            device_id_type=MESH,
        )

    def in_turn(index):
        step = lax.div(index + 1, 2)
        return jnp.where(lax.rem(index, 2) == 1, step, ny - step)

    def y_start(index, carry):
        distance = lax.rem(in_turn(index), ny)
        for side in range(2):
            @pl.when(row_needs(side, lax.rem(y + distance, ny)) & holds(side, band))
            def _():
                y_copy(side, distance).start()

        return carry

    lax.fori_loop(1, ny, y_start, 0)

    def unpack(side, source):
        span = 4 * pairs
        spread[side, pl.ds(pl.multiple_of(source * span, 8), span), :] = blocks[
            side, source
        ].astype(jnp.float32)

    def forward(index, carry):
        source_y = lax.rem(y + in_turn(index), ny)
        for side in range(2):
            held = holds(side, source_y * nx + x)

            @pl.when(row_needs(side, y) & (index > 0) & held)
            def _():
                y_arrival(side, source_y).wait_recv()

            for distance in range(1, nx):
                @pl.when(needs(side, at_x(x + distance)) & held)
                def _():
                    x_copy(side, source_y, distance).start()

            @pl.when(needs(side, band) & held)
            def _():
                unpack(side, source_y * nx + x)

        return carry

    lax.fori_loop(0, ny, forward, 0)

    def collect(index, carry):
        source_y = lax.rem(y + in_turn(index), ny)
        for side in range(2):
            for distance in range(1, nx):
                source = source_y * nx + lax.rem(x + distance, nx)

                @pl.when(needs(side, band) & holds(side, source))
                def _():
                    x_arrival(side, source).wait_recv()
                    unpack(side, source)

        return carry

    lax.fori_loop(0, ny, collect, 0)

    def legendre(sides):
        unroll = 4 if pairs % 4 == 0 else 1

        def some(index, carry):
            for step in range(unroll):
                pair = index * unroll + step
                total = None
                for side in sides:
                    parts = [
                        spread[
                            side, pl.ds((2 * parity + q) * pairs + pair, bands, stride=4 * pairs), :
                        ]
                        for parity in range(2)
                        for q in range(2)
                    ]
                    values = jnp.concatenate(parts, axis=0).astype(jnp.bfloat16)
                    result = jnp.dot(
                        weights[side, pair], values, preferred_element_type=jnp.float32
                    )[:slots]
                    total = result if total is None else total + result
                out_ref[pair] = total
            return carry

        lax.fori_loop(0, pairs // unroll, some, 0)

    pl.when(needs(0, band) & ~needs(1, band))(lambda: legendre((0,)))
    pl.when(needs(1, band) & ~needs(0, band))(lambda: legendre((1,)))
    pl.when(needs(1, band) & needs(0, band))(lambda: legendre((0, 1)))

    sum_copy(False, 0, 0).wait_send()
    sum_copy(True, 0, 1).wait_send()

    for stage in range(stages):
        for side in range(2):
            term_copy(side == 0, stage).wait_send()
            for q in range(2):
                if stage:
                    sum_copy(side == 0, stage, q).wait_send()

    def y_sent(distance, carry):
        for side in range(2):
            @pl.when(row_needs(side, lax.rem(y + distance, ny)) & holds(side, band))
            def _():
                y_copy(side, distance).wait_send()

        return carry

    lax.fori_loop(1, ny, y_sent, 0)

    def x_sent(source_y, carry):
        for side in range(2):
            for distance in range(1, nx):
                @pl.when(needs(side, at_x(x + distance)) & holds(side, source_y * nx + x))
                def _():
                    x_copy(side, source_y, distance).wait_send()

        return carry

    lax.fori_loop(0, ny, x_sent, 0)


def shards(nx, grid, row_points, legendre):
    bands, sets = lax.axis_size("band"), lax.axis_size("set")
    pairs, rows, width = legendre.shape
    slots = width // bands
    per_device = grid.shape[1]
    points = jnp.transpose(grid, (1, 0, 2))
    stages = sets // 8
    padded = -(-slots // 16) * 16
    group_rows = 2 * pairs
    f32, bf16 = jnp.float32, jnp.bfloat16
    table = pltpu.VMEM((2, 2, group_rows, 256), f32)
    early = min(2, stages)
    early_sums = pltpu.VMEM((2, early, 2, 2 * group_rows, 128), bf16)
    sums = pltpu.VMEM((2, max(stages - early, 1), 2, 2 * group_rows, 128), f32)
    terms = pltpu.VMEM((2, stages, 2, 2 * group_rows, 128), bf16)
    return pl.pallas_call(
        functools.partial(kernel, (bands, sets, nx, pairs, slots, per_device)),
        out_shape=jax.ShapeDtypeStruct((pairs, slots, 128), f32),
        in_specs=[
            pl.BlockSpec(memory_space=pltpu.HBM),
            pl.BlockSpec(memory_space=pltpu.HBM),
            pl.BlockSpec(memory_space=pltpu.HBM),
        ],
        out_specs=pl.BlockSpec(memory_space=pltpu.VMEM),
        scratch_shapes=[
            pltpu.SMEM((2,), jnp.int32),
            pltpu.VMEM((per_device, 2, 128), f32),
            pltpu.VMEM((per_device, 2, 128), f32),
            pltpu.VMEM((2, 256, 128), f32),
            pltpu.VMEM((2, 2, 256, 128), bf16),
            pltpu.VMEM((2, 2, 256, 128), bf16),
            pltpu.VMEM((pairs, rows, WINDOW), bf16),
            pltpu.VMEM((rows, 128), f32),
            pltpu.VMEM((2, pairs, padded, 2 * rows), bf16),
            table,
            table,
            early_sums,
            early_sums,
            sums,
            sums,
            terms,
            terms,
            pltpu.VMEM((2, 4 * pairs, 128), f32),
            pltpu.VMEM((2, bands, 4 * pairs, 128), bf16),
            pltpu.VMEM((2, bands * 4 * pairs, 128), f32),
            pltpu.SemaphoreType.DMA,
            pltpu.SemaphoreType.DMA((2,)),
            pltpu.SemaphoreType.DMA((2,)),
            pltpu.SemaphoreType.DMA((2, stages, 2)),
            pltpu.SemaphoreType.DMA((2, stages, 2)),
            pltpu.SemaphoreType.DMA((2, stages)),
            pltpu.SemaphoreType.DMA((2, stages)),
            pltpu.SemaphoreType.DMA((2, bands // nx)),
            pltpu.SemaphoreType.DMA((2, bands // nx)),
            pltpu.SemaphoreType.DMA((2, bands // nx, nx)),
            pltpu.SemaphoreType.DMA((2, bands)),
        ],
        compiler_params=pltpu.CompilerParams(
            collective_id=0, has_side_effects=True, vmem_limit_bytes=62900000
        ),
    )(row_points, points, legendre)


def solution(mesh, nx=CHIPS_X):
    return jax.shard_map(
        functools.partial(shards, nx),
        mesh=mesh,
        in_specs=(P("band", "set", None), P("band"), P("set", None, None)),
        out_specs=P("set", "band", None),
        check_vma=False,
    )
```

```python
import functools
import math

import jax
import jax.numpy as jnp
from jax import lax
from jax.experimental import pallas as pl
from jax.experimental.pallas import tpu as pltpu
from jax.sharding import PartitionSpec as P

MESH = pl.DeviceIdType.MESH
CHIPS_X = 4
WINDOW = 256
SIN_TERMS = (1.0, -1 / 6, 1 / 120, -1 / 5040, 1 / 362880, -1 / 39916800)
COS_TERMS = (1.0, -1 / 2, 1 / 24, -1 / 720, 1 / 40320, -1 / 3628800, 1 / 479001600)


def horner(terms, square):
    total = jnp.full_like(square, terms[-1])
    for term in terms[-2::-1]:
        total = total * square + term
    return total


def cos_sin(waves, points, length):
    product = waves * points
    residue = product - jnp.floor(product * (1.0 / length) + 0.5) * length
    half = residue * (math.pi / length)
    square = half * half
    sine = half * horner(SIN_TERMS, square)
    cosine = horner(COS_TERMS, square)
    return 1.0 - 2.0 * sine * sine, 2.0 * sine * cosine


def split(value):
    high = value.astype(jnp.bfloat16)
    return high, (value - high.astype(jnp.float32)).astype(jnp.bfloat16)


def kernel(
    sizes,
    rows_hbm,
    grid_hbm,
    leg_ref,
    out_ref,
    rows_ref,
    mine_raw,
    twin,
    folded,
    grid_high,
    grid_low,
    window,
    leg_rows,
    weights,
    base_cos,
    base_sin,
    early_out,
    early_in,
    sum_out,
    sum_in,
    term_out,
    term_in,
    packed,
    blocks,
    spread,
    leg_sem,
    own_sem,
    twin_sem,
    sum_send,
    sum_recv,
    term_send,
    term_recv,
    y_send,
    y_recv,
    x_send,
    x_recv,
):
    bands, sets, nx, pairs, slots, per_device = sizes
    ny, nz = bands // nx, sets // 2
    half = nz // 2
    stages = half // 2
    early = early_in.shape[1]
    trunc = 2 * pairs * sets - 1
    group_rows = 2 * pairs
    band, group = lax.axis_index("band"), lax.axis_index("set")
    y, x = lax.div(band, nx), lax.rem(band, nx)
    z, core = lax.div(group, 2), lax.rem(group, 2)
    sibling = z * 2 + 1 - core

    def at_z(position):
        return lax.rem(position + nz, nz) * 2 + core


    def at_y(position):
        return lax.rem(position + ny, ny) * nx + x

    def at_x(position):
        return y * nx + lax.rem(position, nx)

    def needs(side, of_band):
        if side == 0:
            return slots * of_band <= trunc - pairs * group
        return slots * of_band + slots - 1 >= trunc + 1 - (pairs * group + pairs - 1)

    def row_needs(side, of_y):
        return needs(side, of_y * nx + (0 if side == 0 else nx - 1))

    stride = (trunc + 1) // (2 * bands)

    def holds(side, of_band):
        lowest = pairs * group if side == 0 else trunc - pairs * group - (pairs - 1)
        return lowest <= 4 * stride * (of_band + 1) + 7

    peers = [(band, sibling)] + [(band, at_z(z + d)) for d in (1, -1, 2, -2)]
    if nz == 4:
        peers.pop()
    peers += [(at_y(y + d), group) for d in range(1, ny)]
    peers += [(at_x(x + d), group) for d in range(1, nx)]
    barrier = pltpu.get_barrier_semaphore()
    for peer in peers:
        pl.semaphore_signal(barrier, inc=1, device_id=peer, device_id_type=MESH)

    first = slots * band
    start = jnp.minimum(lax.div(first, 128) * 128, leg_ref.shape[2] - WINDOW)
    leg_copy = pltpu.make_async_copy(
        leg_ref.at[:, :, pl.ds(pl.multiple_of(start, 128), WINDOW)], window, leg_sem
    )
    leg_copy.start()
    rows_copy = pltpu.make_async_copy(rows_hbm, rows_ref, own_sem.at[0])
    rows_copy.start()
    grid_copy = pltpu.make_async_copy(
        grid_hbm, mine_raw.at[pl.ds(0, per_device)], own_sem.at[1]
    )
    grid_copy.start()
    folded[:, per_device:, :] = jnp.zeros_like(folded[:, per_device:, :])
    swap = pltpu.make_async_remote_copy(
        src_ref=grid_hbm,
        dst_ref=twin.at[pl.ds(0, per_device)],
        send_sem=twin_sem.at[0],
        recv_sem=twin_sem.at[1],
        device_id=(band, sibling),
        device_id_type=MESH,
    )
    rows_copy.wait()
    lengths = [rows_ref[q].astype(jnp.float32) for q in range(2)]
    bases = [group * per_device, sibling * per_device]

    def prepare(source, half_index):
        for q in range(2):
            folded[q, 0:per_device, :] = source[0:per_device, q, :]
        for q in range(2):
            value = folded[q]
            point = bases[half_index] + lax.broadcasted_iota(jnp.int32, value.shape, 0)
            lane = lax.broadcasted_iota(jnp.int32, value.shape, 1)
            other = pltpu.roll(value, 64, 1)
            value = jnp.where(lane < 64, value + other, other - value)
            value = value * lax.rsqrt(jnp.full(value.shape, lengths[q], jnp.float32))
            row = lax.broadcasted_iota(jnp.int32, value.shape, 0)
            value = jnp.where((point < rows_ref[q]) & (row < per_device), value, 0.0)
            grid_high[q, half_index], grid_low[q, half_index] = split(value)

    def base_tables():
        index = lax.broadcasted_iota(jnp.int32, (group_rows, 256), 0)
        waves = jnp.where(index < pairs, index, trunc - (index - pairs)).astype(jnp.float32)
        lane = lax.broadcasted_iota(jnp.int32, (group_rows, 256), 1)
        for q in range(2):
            length = jnp.full((group_rows, 256), lengths[q], jnp.float32)
            for half_index in range(2):
                points = (bases[half_index] + lane).astype(jnp.float32)
                cosine, sine = cos_sin(waves, points, length)
                base_cos[q, half_index] = cosine
                base_sin[q, half_index] = sine

    def partials(owners):
        count = len(owners) * group_rows
        lane = lax.broadcasted_iota(jnp.int32, (8, 256), 1)
        upward = lax.broadcasted_iota(jnp.int32, (group_rows, 256), 0) < pairs
        results = []
        for q in range(2):
            length = jnp.full((8, 256), lengths[q], jnp.float32)
            total = jnp.zeros((2 * count, 128), jnp.float32)
            for half_index in range(2):
                points = (bases[half_index] + lane).astype(jnp.float32)
                cosine, sine = base_cos[q, half_index], base_sin[q, half_index]
                cosines, sines = [], []
                for owner in owners:
                    waves = jnp.full((8, 256), pairs * owner, jnp.int32).astype(jnp.float32)
                    turn_cos, turn_sin = (
                        jnp.concatenate([part] * (group_rows // 8), axis=0)
                        for part in cos_sin(waves, points, length)
                    )
                    turn_sin = jnp.where(upward, turn_sin, -turn_sin)
                    cosines.append(cosine * turn_cos - sine * turn_sin)
                    sines.append(sine * turn_cos + cosine * turn_sin)
                high, low = split(jnp.concatenate(cosines + sines, axis=0))
                for factor, values in ((high, grid_high), (low, grid_high), (high, grid_low)):
                    total = total + jnp.dot(
                        factor, values[q, half_index], preferred_element_type=jnp.float32
                    )
            results.append(total)
        return results

    def sum_slots(stage):
        return (early_out, early_in, stage) if stage < early else (sum_out, sum_in, stage - early)

    def sum_copy(to_right, stage, q):
        side = 0 if to_right else 1
        source, target, slot = sum_slots(stage)
        return pltpu.make_async_remote_copy(
            src_ref=source.at[side, slot, q],
            dst_ref=target.at[side, slot, q],
            send_sem=sum_send.at[side, stage, q],
            recv_sem=sum_recv.at[side, stage, q],
            device_id=(band, at_z(z + 2 if to_right else z - 2)),
            device_id_type=MESH,
        )

    def term_copy(to_right, stage):
        side = 0 if to_right else 1
        return pltpu.make_async_remote_copy(
            src_ref=term_out.at[side, stage],
            dst_ref=term_in.at[side, stage],
            send_sem=term_send.at[side, stage],
            recv_sem=term_recv.at[side, stage],
            device_id=(band, at_z(z + 1 if to_right else z - 1)),
            device_id_type=MESH,
        )

    def weights_of(pair):
        values = window[pair].astype(jnp.float32)
        values = pltpu.roll(values, lax.rem(WINDOW - (first - start), WINDOW), 1)[:, :128]
        leg_rows[0 : values.shape[0], :] = values
        rows = jnp.concatenate([leg_rows[pl.ds(q, bands, stride=2), :] for q in range(2)], axis=0)
        turned = jnp.transpose(rows)[: weights.shape[2]]
        turned = jnp.concatenate([turned, turned], axis=1)
        slot = first + lax.broadcasted_iota(jnp.int32, turned.shape, 0)
        parity = lax.div(lax.broadcasted_iota(jnp.int32, turned.shape, 1), 2 * bands)
        number = pairs * group + pair
        is_first = slot <= trunc - number
        even = (slot & 1) == parity
        other = ((slot - 1 - trunc + number) & 1) == parity
        weights[0, pair] = jnp.where(is_first & even, turned, 0.0).astype(jnp.bfloat16)
        weights[1, pair] = jnp.where((~is_first) & other, turned, 0.0).astype(jnp.bfloat16)

    base_tables()
    pl.semaphore_wait(barrier, len(peers))
    swap.start()
    grid_copy.wait()
    prepare(mine_raw, 0)
    swap.wait()
    prepare(twin, 1)

    far = partials([at_z(z + half)])
    first_out = sum_slots(0)[0]
    first_out[1, 0, 0] = far[0].astype(first_out.dtype)
    sum_copy(False, 0, 0).start()
    first_out[0, 0, 1] = far[1].astype(first_out.dtype)
    sum_copy(True, 0, 1).start()
    per_step = -(-pairs // max(stages - 1, 1))

    def weights_step(step):
        if step == 1:
            leg_copy.wait()
            spread[...] = jnp.zeros_like(spread)

        def one(index, carry):
            pair = (step - 1) * per_step + index

            @pl.when(pair < pairs)
            def _():
                weights_of(pair)

            return carry

        lax.fori_loop(0, per_step, one, 0)

    def send_terms(stage):
        distance = half - 2 * stage - 1
        terms = partials([at_z(z + distance), at_z(z - distance)])
        for side in range(2):
            for q in range(2):
                for part in range(2):
                    low = (2 * part + side) * group_rows
                    term_out[side, stage, q, part * group_rows : (part + 1) * group_rows] = terms[
                        q
                    ][low : low + group_rows].astype(term_out.dtype)
            term_copy(side == 0, stage).start()

    send_terms(0)

    for stage in range(1, stages):
        send_terms(stage)
        distance = half - 2 * stage
        mine = partials([at_z(z + distance), at_z(z - distance)])
        for side in range(2):
            term_copy(side == 0, stage - 1).wait_recv()
        source, _, slot = sum_slots(stage)
        _, came, came_slot = sum_slots(stage - 1)
        for q in range(2):
            for side in range(2):
                has_sum = stage > 1 or q == 1 - side
                if has_sum:
                    sum_copy(side == 0, stage - 1, q).wait_recv()
                for part in range(2):
                    low = (2 * part + side) * group_rows
                    span = slice(part * group_rows, (part + 1) * group_rows)
                    total = mine[q][low : low + group_rows]
                    total = total + term_in[side, stage - 1, q, span].astype(jnp.float32)
                    if has_sum:
                        total = total + came[side, came_slot, q, span].astype(jnp.float32)
                    source[side, slot, q, span] = total.astype(source.dtype)
                sum_copy(side == 0, stage, q).start()
        weights_step(stage)
    if stages == 1:
        weights_step(1)

    own = partials([group])
    last = stages - 1
    for side in range(2):
        term_copy(side == 0, last).wait_recv()
    for q in range(2):
        for side in range(2):
            if stages > 1 or q == 1 - side:
                sum_copy(side == 0, last, q).wait_recv()

    for q in range(2):
        total = own[q]
        _, came, slot = sum_slots(last)
        for side in range(2):
            total = total + term_in[side, last, q].astype(jnp.float32)
            if stages > 1 or q == 1 - side:
                total = total + came[side, slot, q].astype(jnp.float32)
        index = lax.broadcasted_iota(jnp.int32, (group_rows, 128), 0)
        wave = jnp.where(index < pairs, pairs * group + index, trunc - pairs * group - (index - pairs))
        usable = wave <= lax.div(rows_ref[q] - 1, 2)
        cosine = jnp.where(usable, total[:group_rows], 0.0)
        sine = jnp.where(usable, -total[group_rows:], 0.0)
        lane = lax.broadcasted_iota(jnp.int32, (group_rows, 128), 1)
        parts = (
            jnp.where(lane < 64, cosine, pltpu.roll(sine, 64, 1)),
            jnp.where(lane < 64, pltpu.roll(cosine, 64, 1), sine),
        )
        for parity in range(2):
            for side in range(2):
                at = (parity * 2 + q) * pairs
                packed[side, at : at + pairs] = parts[parity][side * pairs : (side + 1) * pairs]
    for side in range(2):
        blocks[side, band] = packed[side, 0 : 4 * pairs].astype(jnp.bfloat16)

    def y_copy(side, distance):
        return pltpu.make_async_remote_copy(
            src_ref=blocks.at[side, band],
            dst_ref=blocks.at[side, band],
            send_sem=y_send.at[side, distance],
            recv_sem=y_recv.at[side, y],
            device_id=(at_y(y + distance), group),
            device_id_type=MESH,
        )

    def y_arrival(side, source_y):
        spot = blocks.at[side, source_y * nx + x]
        return pltpu.make_async_remote_copy(
            src_ref=spot,
            dst_ref=spot,
            send_sem=y_send.at[side, 0],
            recv_sem=y_recv.at[side, source_y],
            device_id=(at_y(y + 1), group),
            device_id_type=MESH,
        )

    def x_copy(side, source_y, distance):
        spot = blocks.at[side, source_y * nx + x]
        return pltpu.make_async_remote_copy(
            src_ref=spot,
            dst_ref=spot,
            send_sem=x_send.at[side, source_y, distance],
            recv_sem=x_recv.at[side, source_y * nx + x],
            device_id=(at_x(x + distance), group),
            device_id_type=MESH,
        )

    def x_arrival(side, source):
        spot = blocks.at[side, source]
        return pltpu.make_async_remote_copy(
            src_ref=spot,
            dst_ref=spot,
            send_sem=x_send.at[side, 0, 0],
            recv_sem=x_recv.at[side, source],
            device_id=(at_x(x + 1), group),
            device_id_type=MESH,
        )

    def in_turn(index):
        step = lax.div(index + 1, 2)
        return jnp.where(lax.rem(index, 2) == 1, step, ny - step)

    def y_start(index, carry):
        distance = lax.rem(in_turn(index), ny)
        for side in range(2):
            @pl.when(row_needs(side, lax.rem(y + distance, ny)) & holds(side, band))
            def _():
                y_copy(side, distance).start()

        return carry

    lax.fori_loop(1, ny, y_start, 0)

    def unpack(side, source):
        span = 4 * pairs
        spread[side, pl.ds(pl.multiple_of(source * span, 8), span), :] = blocks[
            side, source
        ].astype(jnp.float32)

    def forward(index, carry):
        source_y = lax.rem(y + in_turn(index), ny)
        for side in range(2):
            held = holds(side, source_y * nx + x)

            @pl.when(row_needs(side, y) & (index > 0) & held)
            def _():
                y_arrival(side, source_y).wait_recv()

            for distance in range(1, nx):
                @pl.when(needs(side, at_x(x + distance)) & held)
                def _():
                    x_copy(side, source_y, distance).start()

            @pl.when(needs(side, band) & held)
            def _():
                unpack(side, source_y * nx + x)

        return carry

    lax.fori_loop(0, ny, forward, 0)

    def collect(index, carry):
        source_y = lax.rem(y + in_turn(index), ny)
        for side in range(2):
            for distance in range(1, nx):
                source = source_y * nx + lax.rem(x + distance, nx)

                @pl.when(needs(side, band) & holds(side, source))
                def _():
                    x_arrival(side, source).wait_recv()
                    unpack(side, source)

        return carry

    lax.fori_loop(0, ny, collect, 0)

    def legendre(sides):
        unroll = 4 if pairs % 4 == 0 else 1

        def some(index, carry):
            for step in range(unroll):
                pair = index * unroll + step
                total = None
                for side in sides:
                    parts = [
                        spread[
                            side, pl.ds((2 * parity + q) * pairs + pair, bands, stride=4 * pairs), :
                        ]
                        for parity in range(2)
                        for q in range(2)
                    ]
                    values = jnp.concatenate(parts, axis=0).astype(jnp.bfloat16)
                    result = jnp.dot(
                        weights[side, pair], values, preferred_element_type=jnp.float32
                    )[:slots]
                    total = result if total is None else total + result
                out_ref[pair] = total
            return carry

        lax.fori_loop(0, pairs // unroll, some, 0)

    pl.when(needs(0, band) & ~needs(1, band))(lambda: legendre((0,)))
    pl.when(needs(1, band) & ~needs(0, band))(lambda: legendre((1,)))
    pl.when(needs(1, band) & needs(0, band))(lambda: legendre((0, 1)))

    sum_copy(False, 0, 0).wait_send()
    sum_copy(True, 0, 1).wait_send()

    for stage in range(stages):
        for side in range(2):
            term_copy(side == 0, stage).wait_send()
            for q in range(2):
                if stage:
                    sum_copy(side == 0, stage, q).wait_send()

    def y_sent(distance, carry):
        for side in range(2):
            @pl.when(row_needs(side, lax.rem(y + distance, ny)) & holds(side, band))
            def _():
                y_copy(side, distance).wait_send()

        return carry

    lax.fori_loop(1, ny, y_sent, 0)

    def x_sent(source_y, carry):
        for side in range(2):
            for distance in range(1, nx):
                @pl.when(needs(side, at_x(x + distance)) & holds(side, source_y * nx + x))
                def _():
                    x_copy(side, source_y, distance).wait_send()

        return carry

    lax.fori_loop(0, ny, x_sent, 0)


def shards(nx, grid, row_points, legendre):
    bands, sets = lax.axis_size("band"), lax.axis_size("set")
    pairs, rows, width = legendre.shape
    slots = width // bands
    per_device = grid.shape[1]
    points = jnp.transpose(grid, (1, 0, 2))
    stages = sets // 8
    padded = -(-slots // 16) * 16
    group_rows = 2 * pairs
    f32, bf16 = jnp.float32, jnp.bfloat16
    table = pltpu.VMEM((2, 2, group_rows, 256), f32)
    early = min(2, stages)
    early_sums = pltpu.VMEM((2, early, 2, 2 * group_rows, 128), bf16)
    sums = pltpu.VMEM((2, max(stages - early, 1), 2, 2 * group_rows, 128), f32)
    terms = pltpu.VMEM((2, stages, 2, 2 * group_rows, 128), bf16)
    return pl.pallas_call(
        functools.partial(kernel, (bands, sets, nx, pairs, slots, per_device)),
        out_shape=jax.ShapeDtypeStruct((pairs, slots, 128), f32),
        in_specs=[
            pl.BlockSpec(memory_space=pltpu.HBM),
            pl.BlockSpec(memory_space=pltpu.HBM),
            pl.BlockSpec(memory_space=pltpu.HBM),
        ],
        out_specs=pl.BlockSpec(memory_space=pltpu.VMEM),
        scratch_shapes=[
            pltpu.SMEM((2,), jnp.int32),
            pltpu.VMEM((-(-per_device // 8) * 8, 2, 128), f32),
            pltpu.VMEM((-(-per_device // 8) * 8, 2, 128), f32),
            pltpu.VMEM((2, 256, 128), f32),
            pltpu.VMEM((2, 2, 256, 128), bf16),
            pltpu.VMEM((2, 2, 256, 128), bf16),
            pltpu.VMEM((pairs, rows, WINDOW), bf16),
            pltpu.VMEM((rows + 8, 128), f32),
            pltpu.VMEM((2, pairs, padded, 2 * rows), bf16),
            table,
            table,
            early_sums,
            early_sums,
            sums,
            sums,
            terms,
            terms,
            pltpu.VMEM((2, 4 * pairs + 8, 128), f32),
            pltpu.VMEM((2, bands, 4 * pairs, 128), bf16),
            pltpu.VMEM((2, (bands + 1) * 4 * pairs, 128), f32),
            pltpu.SemaphoreType.DMA,
            pltpu.SemaphoreType.DMA((2,)),
            pltpu.SemaphoreType.DMA((2,)),
            pltpu.SemaphoreType.DMA((2, stages, 2)),
            pltpu.SemaphoreType.DMA((2, stages, 2)),
            pltpu.SemaphoreType.DMA((2, stages)),
            pltpu.SemaphoreType.DMA((2, stages)),
            pltpu.SemaphoreType.DMA((2, bands // nx)),
            pltpu.SemaphoreType.DMA((2, bands // nx)),
            pltpu.SemaphoreType.DMA((2, bands // nx, nx)),
            pltpu.SemaphoreType.DMA((2, bands)),
        ],
        compiler_params=pltpu.CompilerParams(
            collective_id=0, has_side_effects=True, vmem_limit_bytes=62900000
        ),
    )(row_points, points, legendre)


def solution(mesh, nx=CHIPS_X):
    return jax.shard_map(
        functools.partial(shards, nx),
        mesh=mesh,
        in_specs=(P("band", "set", None), P("band"), P("set", None, None)),
        out_specs=P("set", "band", None),
        check_vma=False,
    )
```
